32 devices in a mesh: scen: 4 (over y, x), col: 8 (over z, core).
Axes of the slice: x: 2, y: 2, z: 4, core: 2. Of those that a mesh axis runs over, the one named last changes fastest.
Arguments:
- border: float32 [8, 2048, 16384], P('scen', None, 'col'), may hold values from -0.046875 to 0.046875
- pattern: int32 [8, 16, 128], P('scen', None, 'col'), may hold values 0 or 1
- slack: float32 [8, 2048], P('scen'), may hold values from 0.5 to 2
- first_diag: float32 [16384], P('col'), may hold values from 0.25 to 1.75
- rhs: float32 [16384, 256], P('col'), may hold values from -6 to 6
- scen_rhs: float32 [8, 2048, 256], P('scen', 'col'), may hold values from -6 to 6
Outputs:
- reduced: float32 [8, 2048, 256], P('col', 'scen')
- directions: float32 [8, 2048, 256], P('scen', 'col')
The draws below stay inside these ranges and needn't reach their ends.
All inputs are finite; a program needn't handle non-finite values. No bound on the sum of `pattern` on one device may be relied on, other than what follows from the above.
Results may differ from the reference program's by a relative error of at most 0.0001.
Values sent between devices are 32-bit elements; how exact they have to be, the bound alone decides.
A program may use at most 192 MiB of HBM per device.

```python
import math
import jax
import jax.numpy as jnp
from jax import lax

N0 = 16384
PW = 512
NRHS = 256
ROWS = 2048
ROW_BLOCK = 128
COL_BLOCK = 128
SCEN_ALL = 8
FS_DEV = 2048
N_COL = 8


def draw_border(key, part):
    key_parts = jax.random.split(jax.random.fold_in(key, 7), 3)
    entry_scale = 1.0 / math.sqrt(SCEN_ALL * ROWS)
    separate = jax.random.normal(key_parts[0], (SCEN_ALL, ROWS, N0), jnp.float32)
    common_share = 0.2
    shared_rows = jax.random.normal(key_parts[1], (SCEN_ALL, ROWS, 1), jnp.float32)
    loading = jax.random.uniform(key_parts[2], (1, 1, N0), jnp.float32, 0.6, 1.4)
    mixture = math.sqrt(common_share) * shared_rows * loading + math.sqrt(1.0 - common_share) * separate
    limit_value = 5.9 * entry_scale
    return jnp.clip(entry_scale * mixture, -limit_value, limit_value).astype(jnp.float32)


def set_ends(entries, key, least, top_value):
    shape = entries.shape
    spot = [jax.random.randint(jax.random.fold_in(key, axis), (), 0, shape[axis]) for axis in range(len(shape))]
    entries = entries.at[tuple(spot)].set(least)
    longest = shape.index(max(shape))
    spot[longest] = (spot[longest] + 1) % shape[longest]
    return entries.at[tuple(spot)].set(top_value)


def steps_of(rng, extent, shards, low, largest):
    def one(position, blocks):
        draws = jax.random.uniform(jax.random.fold_in(jax.random.fold_in(rng, 6), position), (blocks,), jnp.float32, low / len(shards), largest / len(shards))
        return jnp.repeat(jnp.exp(draws), extent[position] // blocks).reshape((-1,) + (1,) * (len(extent) - position - 1))

    gain = one(*shards[0])
    for cut in shards[1:]:
        gain = gain * one(*cut)
    return gain


def gaussian(stream_key, extent, spread, reach, cuts=(), kind=jnp.bfloat16):
    array = jax.random.normal(stream_key, extent, jnp.float32) * spread
    if len(cuts) > 0:
        array = steps_of(stream_key, extent, cuts, -0.22, 0.18) * array
    return jnp.clip(array, min=-reach, max=reach).astype(kind)


def setup_inputs(seed: int = 0) -> dict:
    arg_keys = jax.random.split(jax.random.key(seed), 7)
    return {
        "border": draw_border(jax.random.fold_in(arg_keys[6], 71), 0),
        "pattern": set_ends((jax.random.randint(arg_keys[1], (SCEN_ALL, ROWS // ROW_BLOCK, N0 // COL_BLOCK), 0, 4) < 3).astype(jnp.int32), jax.random.fold_in(arg_keys[1], 1), 0, 1),
        "slack": jnp.clip(jnp.exp(math.log(2.0) - 1.3862944 * jax.random.uniform(arg_keys[2], (SCEN_ALL, ROWS), jnp.float32) ** steps_of(arg_keys[2], (SCEN_ALL, ROWS), ((0, 4),), -0.2, 0.2)), 0.5, 2.0),
        "first_diag": jnp.clip(1.0 + 0.15 * jax.random.normal(arg_keys[3], (N0,), jnp.float32), 0.25, 1.75),
        "rhs": gaussian(arg_keys[4], (N0, NRHS), 1.0, 6.0, ((0, 8),), jnp.float32),
        "scen_rhs": gaussian(arg_keys[5], (SCEN_ALL, ROWS, NRHS), 1.0, 6.0, ((0, 4), (1, 8)), jnp.float32),
    }


def expand(block_mask):
    ones = jnp.repeat(block_mask.astype(jnp.float32), ROW_BLOCK, axis=0)
    return jnp.repeat(ones, COL_BLOCK, axis=1)

def panel_index():
    order = jnp.arange(PW, dtype=jnp.int32)
    width_each = PW // N_COL
    return (order // width_each * (N0 // N_COL) + order % width_each).astype(jnp.int32)

def reference(border, pattern, slack, first_diag, rhs, scen_rhs):
    chosen = panel_index()
    order = jnp.arange(PW, dtype=jnp.int32)

    def accumulate(running, members):
        block_rows, block_mask, barrier = members
        masked = block_rows * expand(block_mask)
        panel_part = masked[:, chosen] / barrier[:, None]
        added = jnp.dot(masked.T.astype(jnp.float32), panel_part.astype(jnp.float32), precision=lax.Precision.HIGHEST, preferred_element_type=jnp.float32)
        return (running + added, None)
    schur, _ = lax.scan(accumulate, jnp.zeros((N0, PW), jnp.float32), (border, pattern, slack))
    schur = schur.at[chosen, order].add(first_diag[chosen])
    factor = jnp.linalg.cholesky(schur[chosen])
    forward = lax.linalg.triangular_solve(factor, rhs[chosen], left_side=True, lower=True)
    solved = lax.linalg.triangular_solve(factor, forward, left_side=True, lower=True, transpose_a=True)
    reduced = rhs - jnp.dot(schur.astype(jnp.float32), solved.astype(jnp.float32), precision=lax.Precision.HIGHEST, preferred_element_type=jnp.float32)
    reduced = reduced.at[chosen].set(forward)

    def direction(members):
        block_rows, block_mask, barrier, second_rhs = members
        panel_part = (block_rows * expand(block_mask))[:, chosen]
        moved = jnp.dot(panel_part.astype(jnp.float32), solved.astype(jnp.float32), precision=lax.Precision.HIGHEST, preferred_element_type=jnp.float32)
        return (second_rhs - moved) / barrier[:, None]
    directions = lax.map(direction, (border, pattern, slack, scen_rhs))
    return (reduced.reshape(N0 // FS_DEV, FS_DEV, NRHS), directions)
```

```python
import functools

import jax
import jax.numpy as jnp
from jax import lax
from jax.experimental import pallas as pl
from jax.experimental.pallas import tpu as pltpu
from jax.sharding import PartitionSpec as P

PW = 512
BLK = 128
HIGHEST = lax.Precision.HIGHEST


def dot(a, b, contract=((1,), (0,))):
    return lax.dot_general(
        a, b, (contract, ((), ())), precision=HIGHEST, preferred_element_type=jnp.float32
    )


def invert_factor(block):
    groups = BLK // 8
    shape = (8, BLK)
    sub = lax.broadcasted_iota(jnp.int32, shape, 0)
    lane = lax.broadcasted_iota(jnp.int32, shape, 1)
    rows = [block[8 * i : 8 * i + 8, :] for i in range(groups)]
    inverse = [jnp.where(lane == sub + 8 * i, 1.0, 0.0).astype(jnp.float32) for i in range(groups)]
    for g in range(groups):
        columns = [
            {i: jnp.broadcast_to(rows[i][:, 8 * g + m : 8 * g + m + 1], shape) for i in range(g, groups)}
            for m in range(8)
        ]
        pivots = jnp.ones(shape, jnp.float32)
        for m in range(8):
            head = columns[m][g]
            pivot = jnp.broadcast_to(head[m : m + 1, :], shape)
            scale = 1.0 / pivot
            pivots = jnp.where(sub == m, pivot, pivots)
            row = jnp.broadcast_to(rows[g][m : m + 1, :], shape) * scale
            inverse_row = jnp.broadcast_to(inverse[g][m : m + 1, :], shape) * scale
            factors = [
                jnp.broadcast_to(head[later : later + 1, :], shape) * scale for later in range(m + 1, 8)
            ]
            for i in range(g, groups):
                column = columns[m][i]
                if i == g:
                    column = jnp.where(sub > m, column, 0.0)
                rows[i] = rows[i] - column * row
                inverse[i] = inverse[i] - column * inverse_row
                for later in range(m + 1, 8):
                    columns[later][i] = columns[later][i] - column * factors[later - m - 1]
        inverse[g] = inverse[g] * lax.rsqrt(pivots)
    return jnp.concatenate(inverse, axis=0)


def solve_kernel(packed, rhs, forward, solved, matrix, right, upper, inverses):
    steps = matrix.shape[0] // BLK
    matrix[...] = jnp.zeros_like(matrix)
    offset = 0
    for i in range(steps):
        width = matrix.shape[1] - i * BLK
        matrix[i * BLK : (i + 1) * BLK, i * BLK :] = packed[:, offset : offset + width]
        offset += width
    right[...] = rhs[...]
    solved[...] = jnp.zeros_like(solved)

    def eliminate(j, carry):
        here = pl.ds(pl.multiple_of(j * BLK, BLK), BLK)
        inverse = invert_factor(matrix[here, here])
        inverses[here, :] = inverse
        wide = dot(inverse, matrix[here, :])
        part = dot(inverse, right[here, :])
        cols = lax.broadcasted_iota(jnp.int32, wide.shape, 1)
        wide = jnp.where(cols >= (j + 1) * BLK, wide, 0.0)
        upper[here, :] = wide
        forward[here, :] = part
        matrix[...] -= dot(wide, wide, ((0,), (0,)))
        right[...] -= dot(wide, part, ((0,), (0,)))
        return carry

    lax.fori_loop(0, steps, eliminate, 0)

    def substitute(t, carry):
        here = pl.ds(pl.multiple_of((steps - 1 - t) * BLK, BLK), BLK)
        rest = forward[here, :] - dot(upper[here, :], solved[...])
        solved[here, :] = dot(inverses[here, :], rest, ((0,), (0,)))
        return carry

    lax.fori_loop(0, steps, substitute, 0)


def factor_and_solve(packed, rhs):
    size, width = rhs.shape
    out = jax.ShapeDtypeStruct((size, width), jnp.float32)
    return pl.pallas_call(
        solve_kernel,
        out_shape=(out, out),
        in_specs=[pl.BlockSpec(memory_space=pltpu.VMEM)] * 2,
        out_specs=[pl.BlockSpec(memory_space=pltpu.VMEM)] * 2,
        scratch_shapes=[
            pltpu.VMEM((size, size), jnp.float32),
            pltpu.VMEM((size, width), jnp.float32),
            pltpu.VMEM((size, size), jnp.float32),
            pltpu.VMEM((size, BLK), jnp.float32),
        ],
    )(packed, rhs)


def halves(x):
    high = x.astype(jnp.bfloat16)
    return high, (x - high.astype(jnp.float32)).astype(jnp.bfloat16)


MESH = pl.DeviceIdType.MESH
CHUNKS = 2
STAGES = 4


def tail_kernel(
    mesh_sizes, row_block, solved, forward, panel, slack_col, scen_rhs, mask, border, rhs, reduced, directions,
    stage, high, low, held, split, total, landed, rhs_rows,
    stage_sem, rhs_sem, send_right, send_left, send_core, recv_right, recv_left, recv_core, scen_send, scen_recv,
):
    scen_count, col_count = mesh_sizes
    chips = col_count // 2
    scen = lax.axis_index("scen")
    col = lax.axis_index("col")
    chip, core = col // 2, col % 2
    sibling = chip * 2 + (1 - core)
    scen_local, pw, row_share = panel.shape
    pivot_width = pw // col_count
    own_width = border.shape[2]
    own_share = own_width // scen_count
    rhs_chunk = solved.shape[1] // CHUNKS
    units = scen_local * col_count
    chip_rows = 2 * scen_local * row_share

    def border_copy(unit):
        scenario, owner = unit // col_count, unit % col_count
        slot = unit % STAGES
        return pltpu.make_async_copy(
            border.at[scenario, pl.ds(pl.multiple_of(owner * row_share, row_share), row_share)],
            stage.at[slot],
            stage_sem.at[slot],
        )

    for unit in range(STAGES):
        border_copy(unit).start()
    rhs_copy = pltpu.make_async_copy(
        rhs.at[pl.ds(pl.multiple_of(scen * own_share, own_share), own_share)], rhs_rows, rhs_sem
    )
    rhs_copy.start()

    barrier = pltpu.get_barrier_semaphore()
    pl.semaphore_signal(barrier, inc=1, device_id={"col": sibling}, device_id_type=MESH)
    for d in range(1, scen_count):
        pl.semaphore_signal(
            barrier, inc=1, device_id={"scen": lax.rem(scen + d, scen_count)}, device_id_type=MESH
        )

    @pl.when(chip + 1 < chips)
    def _():
        pl.semaphore_signal(barrier, inc=1, device_id={"col": col + 2}, device_id_type=MESH)

    @pl.when(chip > 0)
    def _():
        pl.semaphore_signal(barrier, inc=1, device_id={"col": col - 2}, device_id_type=MESH)

    ends = jnp.where(chip + 1 < chips, 1, 0) + jnp.where(chip > 0, 1, 0)
    pl.semaphore_wait(barrier, scen_count + ends)

    def hop(q, origin, target, send, recv, lane=core):
        block = held.at[q, origin * 2 + lane]
        return pltpu.make_async_remote_copy(
            src_ref=block,
            dst_ref=block,
            send_sem=send.at[q, origin],
            recv_sem=recv.at[q, origin],
            device_id={"col": target},
            device_id_type=MESH,
        )

    def to_right(q, origin):
        return hop(q, origin, col + 2, send_right, recv_right)

    def to_left(q, origin):
        return hop(q, origin, col - 2, send_left, recv_left)

    def to_sibling(q, origin):
        return hop(q, origin, sibling, send_core, recv_core)

    def from_sibling(q, origin):
        return hop(q, origin, sibling, send_core, recv_core, 1 - core)

    def send_own(q):
        @pl.when(chip + 1 < chips)
        def _():
            to_right(q, chip).start()

        @pl.when(chip > 0)
        def _():
            to_left(q, chip).start()

        to_sibling(q, chip).start()

    def relay(q, distance):
        @pl.when(chip - distance >= 0)
        def _():
            origin = chip - distance
            to_right(q, origin).wait_recv()

            @pl.when(chip + 1 < chips)
            def _():
                to_right(q, origin).start()

            to_sibling(q, origin).start()

        @pl.when(chip + distance < chips)
        def _():
            origin = chip + distance
            to_left(q, origin).wait_recv()

            @pl.when(chip > 0)
            def _():
                to_left(q, origin).start()

            to_sibling(q, origin).start()

    def convert(begin, end):
        def body(unit, carry):
            scenario, owner = unit // col_count, unit % col_count
            slot = unit % STAGES
            place = ((owner // 2 * scen_local + scenario) * 2 + owner % 2) * row_share
            border_copy(unit).wait()
            for r in range(row_share // row_block):
                weight = mask[scenario, owner * (row_share // row_block) + r]

                def some(t, inner):
                    rows = r * row_block + t * 16
                    value = stage[slot, pl.ds(pl.multiple_of(rows, 16), 16), :] * weight
                    top = value.astype(jnp.bfloat16)
                    here = pl.ds(pl.multiple_of(place + rows, 16), 16)
                    high[here, :] = top
                    low[here, :] = (value - top.astype(jnp.float32)).astype(jnp.bfloat16)
                    return inner

                lax.fori_loop(0, row_block // 16, some, 0)

            @pl.when(unit + STAGES < units)
            def _():
                border_copy(unit + STAGES).start()

            return carry

        lax.fori_loop(begin, end, body, 0)

    def own_rows(q):
        lanes = slice(q * rhs_chunk, (q + 1) * rhs_chunk)
        for s in range(scen_local):
            moved = dot(solved[:, lanes], panel[s], ((0,), (0,)))
            held[q, col, s] = moved / slack_col[s]
            directions[s, :, lanes] = moved.T

    def multiply(q, origin, first):
        for s in range(scen_local):
            for k in range(2):
                value = held[q, origin * 2 + k, s]
                top, rest = halves(value)
                lanes = slice((s * 2 + k) * row_share, (s * 2 + k + 1) * row_share)
                split[:rhs_chunk, lanes] = top
                split[rhs_chunk:, lanes] = rest
        width = min(512, own_width)
        rows = pl.ds(pl.multiple_of(origin * chip_rows, chip_rows), chip_rows)

        def body(n, carry):
            lanes = pl.ds(pl.multiple_of(n * width, width), width)
            both = jnp.dot(split[...], high[rows, lanes], preferred_element_type=jnp.float32)
            value = both[:rhs_chunk] + both[rhs_chunk:]
            value += jnp.dot(split[:rhs_chunk], low[rows, lanes], preferred_element_type=jnp.float32)
            if first:
                total[q, :, lanes] = value
            else:
                total[q, :, lanes] += value
            return carry

        lax.fori_loop(0, own_width // width, body, 0)

    def add_in(q, distance):
        if distance == 0:
            from_sibling(q, chip).wait_recv()
            multiply(q, chip, True)
            return

        @pl.when(chip - distance >= 0)
        def _():
            from_sibling(q, chip - distance).wait_recv()
            multiply(q, chip - distance, False)

        @pl.when(chip + distance < chips)
        def _():
            from_sibling(q, chip + distance).wait_recv()
            multiply(q, chip + distance, False)

    def share(q, d):
        peer = lax.rem(scen + d, scen_count)
        return pltpu.make_async_remote_copy(
            src_ref=total.at[q, :, pl.ds(pl.multiple_of(peer * own_share, own_share), own_share)],
            dst_ref=landed.at[q, d - 1],
            send_sem=scen_send.at[q, d - 1],
            recv_sem=scen_recv.at[q, d - 1],
            device_id={"scen": peer},
            device_id_type=MESH,
        )

    def finish(q):
        value = total[q, :, pl.ds(pl.multiple_of(scen * own_share, own_share), own_share)]
        for d in range(1, scen_count):
            share(q, d).wait_recv()
            value += landed[q, d - 1]
        lanes = slice(q * rhs_chunk, (q + 1) * rhs_chunk)
        reduced[:, lanes] = rhs_rows[:, lanes] - value.T

    own_rows(0)
    send_own(0)
    for q in range(1, CHUNKS):
        own_rows(q)
    steps = chips
    for t in range(steps):
        if t > 0:
            relay(0, t)
        convert(t * units // steps, (t + 1) * units // steps)
    rhs_copy.wait()
    for q in range(CHUNKS):
        for distance in range(chips):
            if q + 1 < CHUNKS:
                if distance == 0:
                    send_own(q + 1)
                else:
                    relay(q + 1, distance)
            add_in(q, distance)
        for d in range(1, scen_count):
            share(q, d).start()
        if q == 0:
            for s in range(scen_local):
                directions[s] = (scen_rhs[s] - directions[s]) / slack_col[s].T
        else:
            finish(q - 1)
    finish(CHUNKS - 1)

    @pl.when(scen == 0)
    def _():
        reduced[:pivot_width, :] = forward[pl.ds(pl.multiple_of(col * pivot_width, pivot_width), pivot_width), :]

    for q in range(CHUNKS):
        for origin in range(chips):
            @pl.when((origin <= chip) & (chip + 1 < chips))
            def _():
                to_right(q, origin).wait_send()

            @pl.when((origin >= chip) & (chip > 0))
            def _():
                to_left(q, origin).wait_send()

            to_sibling(q, origin).wait_send()
        for d in range(1, scen_count):
            share(q, d).wait_send()


def tail(solved, forward, panel, slack_rows, scen_rhs, mask, border, rhs, row_block):
    scen_count = lax.axis_size("scen")
    col_count = lax.axis_size("col")
    chips = col_count // 2
    scen_local, _, row_share = panel.shape
    rhs_count = rhs.shape[1]
    _, row_total, own_width = border.shape
    own_share = own_width // scen_count
    rhs_chunk = rhs_count // CHUNKS
    vmem = pl.BlockSpec(memory_space=pltpu.VMEM)
    hbm = pl.BlockSpec(memory_space=pl.ANY)
    dma = pltpu.SemaphoreType.DMA
    return pl.pallas_call(
        functools.partial(tail_kernel, (scen_count, col_count), row_block),
        in_specs=[vmem] * 6 + [hbm] * 2,
        out_specs=[vmem] * 2,
        out_shape=(
            jax.ShapeDtypeStruct((own_share, rhs_count), jnp.float32),
            jax.ShapeDtypeStruct(scen_rhs.shape, jnp.float32),
        ),
        scratch_shapes=[
            pltpu.VMEM((STAGES, row_share, own_width), jnp.float32),
            pltpu.VMEM((scen_local * row_total, own_width), jnp.bfloat16),
            pltpu.VMEM((scen_local * row_total, own_width), jnp.bfloat16),
            pltpu.VMEM((CHUNKS, col_count, scen_local, rhs_chunk, row_share), jnp.float32),
            pltpu.VMEM((2 * rhs_chunk, 2 * scen_local * row_share), jnp.bfloat16),
            pltpu.VMEM((CHUNKS, rhs_chunk, own_width), jnp.float32),
            pltpu.VMEM((CHUNKS, scen_count - 1, rhs_chunk, own_share), jnp.float32),
            pltpu.VMEM((own_share, rhs_count), jnp.float32),
            dma((STAGES,)),
            dma,
        ]
        + [dma((CHUNKS, chips)) for _ in range(6)]
        + [dma((CHUNKS, scen_count - 1)) for _ in range(2)],
        compiler_params=pltpu.CompilerParams(
            collective_id=1, has_side_effects=True, vmem_limit_bytes=60 << 20
        ),
        cost_estimate=pl.CostEstimate(
            flops=6 * scen_local * row_total * own_width * rhs_count,
            bytes_accessed=4 * scen_local * row_total * own_width,
            transcendentals=0,
        ),
    )(solved, forward, panel, slack_rows, scen_rhs, mask, border, rhs)


def per_device(border, pattern, slack, first_diag, rhs, scen_rhs):
    col_count = lax.axis_size("col")
    col_index = lax.axis_index("col")
    scen_index = lax.axis_index("scen")
    scen_local, row_total, own_width = border.shape
    row_blocks, width_blocks = pattern.shape[1:]
    row_block = row_total // row_blocks
    col_block = own_width // width_blocks
    pivot_width = PW // col_count
    row_share = row_total // col_count

    weights = pattern.astype(jnp.float32)
    row_weights = jnp.repeat(weights, row_block, axis=1)
    panel_weights = jnp.repeat(row_weights[:, :, : -(-pivot_width // col_block)], col_block, axis=2)
    own_panel = border[:, :, :pivot_width] * panel_weights[:, :, :pivot_width]
    sent = own_panel.reshape(scen_local, col_count, row_share, pivot_width).transpose(1, 0, 3, 2)
    got = lax.all_to_all(sent, "col", split_axis=0, concat_axis=0, tiled=True)
    panel = got.transpose(1, 0, 2, 3).reshape(scen_local, PW, row_share)

    slack_rows = lax.dynamic_slice_in_dim(slack, col_index * row_share, row_share, 1)
    inverse_slack = 1.0 / slack_rows
    gram = lax.dot_general(
        panel * inverse_slack[:, None, :],
        panel,
        (((0, 2), (0, 2)), ((), ())),
        precision=HIGHEST,
        preferred_element_type=jnp.float32,
    )
    order = jnp.arange(PW, dtype=jnp.int32)
    mine = (order // pivot_width == col_index) & (scen_index == 0)
    diagonal = jnp.where(mine, jnp.tile(first_diag[:pivot_width], col_count), 0.0)
    gram = gram + jnp.where(order[:, None] == order[None, :], diagonal[:, None], 0.0)
    packed = jnp.concatenate(
        [gram[i * BLK : (i + 1) * BLK, i * BLK :] for i in range(PW // BLK)], axis=1
    )
    pieces = lax.all_to_all(
        packed.reshape(col_count, -1, packed.shape[1]), "col", split_axis=0, concat_axis=0, tiled=True
    )
    piece = lax.all_gather(jnp.sum(pieces, axis=0), "scen", axis=0).sum(axis=0)
    own_rhs = rhs[:pivot_width].reshape(piece.shape[0], -1)
    joined = lax.all_gather(jnp.concatenate([piece, own_rhs], axis=1), "col", axis=0, tiled=True)
    rhs_panel = joined[:, packed.shape[1] :].reshape(PW, rhs.shape[1])
    forward, solved = factor_and_solve(joined[:, : packed.shape[1]], rhs_panel)

    mask = jnp.repeat(weights, col_block, axis=2)[:, :, None, :]
    reduced, directions = tail(
        solved, forward, panel, slack_rows[:, None, :], scen_rhs, mask, border, rhs, row_block
    )
    return reduced[None], directions


def solution(mesh):
    return jax.shard_map(
        per_device,
        mesh=mesh,
        in_specs=(
            P("scen", None, "col"),
            P("scen", None, "col"),
            P("scen", None),
            P("col"),
            P("col", None),
            P("scen", "col", None),
        ),
        out_specs=(P("col", "scen", None), P("scen", "col", None)),
        check_vma=False,
    )
```

```python
import functools

import jax
import jax.numpy as jnp
from jax import lax
from jax.experimental import pallas as pl
from jax.experimental.pallas import tpu as pltpu
from jax.sharding import PartitionSpec as P

PW = 512
BLK = 128
HIGHEST = lax.Precision.HIGHEST
MESH = pl.DeviceIdType.MESH
CHUNKS = 2
STAGES = 4


def dot(a, b, contract=((1,), (0,))):
    return lax.dot_general(
        a, b, (contract, ((), ())), precision=HIGHEST, preferred_element_type=jnp.float32
    )


def blocks_of(steps):
    return [(i, j) for i in range(steps) for j in range(i, steps)]


def panel_kernel(
    mesh_sizes, row_block, slack, mask, diagonal, border, rhs, panel, packed, rhs_panel,
    raw, sent, gram, pair, pieces,
    raw_sem, rhs_sem, out_send, out_recv, rhs_send, rhs_recv, rhs_core_send, rhs_core_recv,
    pair_sems, sum_send, sum_recv, all_send, all_recv, core_sems,
):
    scen_count, col_count = mesh_sizes
    chips = col_count // 2
    places = scen_count * chips
    scen = lax.axis_index("scen")
    col = lax.axis_index("col")
    chip, core = col // 2, col % 2
    sibling = chip * 2 + (1 - core)
    place = scen * chips + chip
    scen_local, pw, row_share = panel.shape
    pivot_width = pw // col_count
    lanes_read = raw.shape[3]
    piece = pieces.shape[1]
    half = piece * places

    def target(t):
        return lax.rem(col + col_count // 2 + t, col_count)

    def rows_of(owner):
        return pl.ds(pl.multiple_of(owner * row_share, row_share), row_share)

    def pivots_of(owner):
        return pl.ds(pl.multiple_of(owner * pivot_width, pivot_width), pivot_width)

    def read(t):
        return pltpu.make_async_copy(
            border.at[:, rows_of(target(t)), pl.ds(0, lanes_read)], raw.at[t], raw_sem.at[t]
        )

    for t in range(col_count):
        read(t).start()
    own_rhs = pltpu.make_async_copy(rhs.at[pl.ds(0, pivot_width)], rhs_panel.at[pivots_of(col)], rhs_sem)
    own_rhs.start()

    barrier = pltpu.get_barrier_semaphore()

    def greet(device):
        pl.semaphore_signal(barrier, inc=1, device_id=device, device_id_type=MESH)

    def away(e):
        other = lax.rem(place + e, places)
        return {"scen": other // chips, "col": lax.rem(other, chips) * 2 + core}

    def across(e):
        return {"col": lax.rem(chip + e, chips) * 2 + (1 - core)}

    for e in range(1, places):
        greet(away(e))
    for e in range(chips):
        greet(across(e))

    def hand_out(t):
        return pltpu.make_async_remote_copy(
            src_ref=sent.at[t],
            dst_ref=panel.at[:, pivots_of(col), :],
            send_sem=out_send.at[t],
            recv_sem=out_recv.at[t],
            device_id={"col": target(t)},
            device_id_type=MESH,
        )

    def hand_in(t):
        source = lax.rem(col + 2 * col_count - col_count // 2 - t, col_count)
        return pltpu.make_async_remote_copy(
            src_ref=sent.at[t],
            dst_ref=panel.at[:, pivots_of(source), :],
            send_sem=out_send.at[t],
            recv_sem=out_recv.at[t],
            device_id={"col": source},
            device_id_type=MESH,
        )

    here = col_count - col_count // 2
    for t in range(col_count):
        read(t).wait()
        for s in range(scen_local):
            for r in range(row_share // row_block):
                weight = mask[s, target(t) * (row_share // row_block) + r, :, :lanes_read]
                value = raw[t, s, r * row_block : (r + 1) * row_block, :] * weight
                value = value.T[:pivot_width]
                if t == here:
                    panel[s, pivots_of(col), r * row_block : (r + 1) * row_block] = value
                else:
                    sent[t, s, :, r * row_block : (r + 1) * row_block] = value
        if t == 0:
            pl.semaphore_wait(barrier, places - 1 + chips)
        if t != here:
            hand_out(t).start()

    def rhs_away(e, origin_shift=0):
        return pltpu.make_async_remote_copy(
            src_ref=rhs_panel.at[pivots_of(col)],
            dst_ref=rhs_panel.at[pivots_of(col)],
            send_sem=rhs_send.at[e - 1],
            recv_sem=rhs_recv.at[e - 1],
            device_id={"col": lax.rem(chip + e, chips) * 2 + core},
            device_id_type=MESH,
        )

    def rhs_from(e):
        source = lax.rem(chip + chips - e, chips) * 2 + core
        return pltpu.make_async_remote_copy(
            src_ref=rhs_panel.at[pivots_of(source)],
            dst_ref=rhs_panel.at[pivots_of(source)],
            send_sem=rhs_send.at[e - 1],
            recv_sem=rhs_recv.at[e - 1],
            device_id={"col": source},
            device_id_type=MESH,
        )

    def rhs_core(e, side):
        owner = lax.rem(chip + chips - e, chips) * 2 + side
        return pltpu.make_async_remote_copy(
            src_ref=rhs_panel.at[pivots_of(owner)],
            dst_ref=rhs_panel.at[pivots_of(owner)],
            send_sem=rhs_core_send.at[e],
            recv_sem=rhs_core_recv.at[e],
            device_id={"col": sibling},
            device_id_type=MESH,
        )

    for t in range(col_count):
        if t != here:
            hand_in(t).wait_recv()

    own_rhs.wait()
    for e in range(1, chips):
        rhs_away(e).start()
    rhs_core(0, core).start()

    steps = pw // BLK
    whole = [panel[s] for s in range(scen_local)]
    scaled = [panel[s] / slack[s, :, rows_of(col)] for s in range(scen_local)]
    whole = jnp.concatenate(whole, axis=1)
    scaled = jnp.concatenate(scaled, axis=1)
    row = lax.broadcasted_iota(jnp.int32, (BLK, BLK), 0)
    lane = lax.broadcasted_iota(jnp.int32, (BLK, BLK), 1)
    index = 0
    for i in range(steps):
        wide = dot(scaled[i * BLK : (i + 1) * BLK], whole[i * BLK :], ((1,), (1,)))
        mine = (row == lane) & ((lane + i * BLK) // pivot_width == col) & (scen == 0)
        for j in range(i, steps):
            value = wide[:, (j - i) * BLK : (j - i + 1) * BLK]
            if i == j:
                value = value + jnp.where(mine, jnp.broadcast_to(diagonal[...], (BLK, BLK)), 0.0)
            gram[index * BLK : (index + 1) * BLK, :] = value
            index += 1
    if index * BLK < gram.shape[0]:
        gram[index * BLK :, :] = jnp.zeros((gram.shape[0] - index * BLK, BLK), jnp.float32)

    def half_of(side):
        return pl.ds(pl.multiple_of(side * half, 8), half)

    swap = pltpu.make_async_remote_copy(
        src_ref=gram.at[half_of(1 - core)],
        dst_ref=pair,
        send_sem=pair_sems.at[0],
        recv_sem=pair_sems.at[1],
        device_id={"col": sibling},
        device_id_type=MESH,
    )
    swap.start()
    swap.wait_recv()
    pair[...] += gram[half_of(core), :]

    def piece_of(index):
        return pl.ds(pl.multiple_of(index * piece, 8), piece)

    def spread(e):
        return pltpu.make_async_remote_copy(
            src_ref=pair.at[piece_of(lax.rem(place + e, places))],
            dst_ref=pieces.at[e - 1],
            send_sem=sum_send.at[e - 1],
            recv_sem=sum_recv.at[e - 1],
            device_id=away(e),
            device_id_type=MESH,
        )

    for e in range(1, places):
        spread(e).start()
    for e in range(1, chips):
        rhs_from(e).wait_recv()
        rhs_core(e, core).start()
    value = pair[piece_of(place), :]
    for e in range(1, places):
        spread(e).wait_recv()
        value += pieces[e - 1]

    def slot_of(index):
        return pl.ds(pl.multiple_of(core * half + index * piece, 8), piece)

    packed[slot_of(place), :] = value

    def collect(e, origin):
        return pltpu.make_async_remote_copy(
            src_ref=packed.at[slot_of(origin)],
            dst_ref=packed.at[slot_of(origin)],
            send_sem=all_send.at[e - 1],
            recv_sem=all_recv.at[e - 1],
            device_id=away(e),
            device_id_type=MESH,
        )

    for e in range(1, places):
        collect(e, place).start()
    for e in range(1, places):
        collect(e, lax.rem(place + places - e, places)).wait_recv()

    def finish(side):
        return pltpu.make_async_remote_copy(
            src_ref=packed.at[half_of(side)],
            dst_ref=packed.at[half_of(side)],
            send_sem=core_sems.at[0],
            recv_sem=core_sems.at[1],
            device_id={"col": sibling},
            device_id_type=MESH,
        )

    finish(core).start()
    for e in range(chips):
        rhs_core(e, 1 - core).wait_recv()
    finish(1 - core).wait_recv()
    for t in range(col_count):
        if t != here:
            hand_out(t).wait_send()
    for e in range(1, chips):
        rhs_away(e).wait_send()
    for e in range(chips):
        rhs_core(e, core).wait_send()
    swap.wait_send()
    for e in range(1, places):
        spread(e).wait_send()
        collect(e, place).wait_send()
    finish(core).wait_send()


def gather_panel(slack, mask, diagonal, border, rhs, row_block):
    scen_count = lax.axis_size("scen")
    col_count = lax.axis_size("col")
    chips = col_count // 2
    places = scen_count * chips
    scen_local, row_total, own_width = border.shape
    row_share = row_total // col_count
    pivot_width = PW // col_count
    rhs_count = rhs.shape[1]
    lanes_read = -(-pivot_width // BLK) * BLK
    count = len(blocks_of(PW // BLK)) * BLK
    piece = -(-count // (2 * places * 8)) * 8
    half = piece * places
    vmem = pl.BlockSpec(memory_space=pltpu.VMEM)
    hbm = pl.BlockSpec(memory_space=pl.ANY)
    dma = pltpu.SemaphoreType.DMA
    return pl.pallas_call(
        functools.partial(panel_kernel, (scen_count, col_count), row_block),
        in_specs=[vmem] * 3 + [hbm] * 2,
        out_specs=[vmem] * 3,
        out_shape=(
            jax.ShapeDtypeStruct((scen_local, PW, row_share), jnp.float32),
            jax.ShapeDtypeStruct((2 * half, BLK), jnp.float32),
            jax.ShapeDtypeStruct((PW, rhs_count), jnp.float32),
        ),
        scratch_shapes=[
            pltpu.VMEM((col_count, scen_local, row_share, lanes_read), jnp.float32),
            pltpu.VMEM((col_count, scen_local, pivot_width, row_share), jnp.float32),
            pltpu.VMEM((2 * half, BLK), jnp.float32),
            pltpu.VMEM((half, BLK), jnp.float32),
            pltpu.VMEM((places - 1, piece, BLK), jnp.float32),
            dma((col_count,)),
            dma,
            dma((col_count,)),
            dma((col_count,)),
            dma((chips - 1,)),
            dma((chips - 1,)),
            dma((chips,)),
            dma((chips,)),
            dma((2,)),
            dma((places - 1,)),
            dma((places - 1,)),
            dma((places - 1,)),
            dma((places - 1,)),
            dma((2,)),
        ],
        compiler_params=pltpu.CompilerParams(
            collective_id=0, has_side_effects=True, vmem_limit_bytes=40 << 20
        ),
        cost_estimate=pl.CostEstimate(
            flops=12 * PW * PW * scen_local * row_share, bytes_accessed=8 << 20, transcendentals=0
        ),
    )(slack, mask, diagonal, border, rhs)


def invert_factor(block):
    groups = BLK // 8
    shape = (8, BLK)
    sub = lax.broadcasted_iota(jnp.int32, shape, 0)
    lane = lax.broadcasted_iota(jnp.int32, shape, 1)
    rows = [block[8 * i : 8 * i + 8, :] for i in range(groups)]
    inverse = [jnp.where(lane == sub + 8 * i, 1.0, 0.0).astype(jnp.float32) for i in range(groups)]
    for g in range(groups):
        columns = [
            {i: jnp.broadcast_to(rows[i][:, 8 * g + m : 8 * g + m + 1], shape) for i in range(g, groups)}
            for m in range(8)
        ]
        pivots = jnp.ones(shape, jnp.float32)
        for m in range(8):
            head = columns[m][g]
            pivot = jnp.broadcast_to(head[m : m + 1, :], shape)
            scale = 1.0 / pivot
            pivots = jnp.where(sub == m, pivot, pivots)
            row = jnp.broadcast_to(rows[g][m : m + 1, :], shape) * scale
            inverse_row = jnp.broadcast_to(inverse[g][m : m + 1, :], shape) * scale
            factors = [
                jnp.broadcast_to(head[later : later + 1, :], shape) * scale for later in range(m + 1, 8)
            ]
            for i in range(g, groups):
                column = columns[m][i]
                if i == g:
                    column = jnp.where(sub > m, column, 0.0)
                rows[i] = rows[i] - column * row
                inverse[i] = inverse[i] - column * inverse_row
                for later in range(m + 1, 8):
                    columns[later][i] = columns[later][i] - column * factors[later - m - 1]
        inverse[g] = inverse[g] * lax.rsqrt(pivots)
    return jnp.concatenate(inverse, axis=0)


def solve_kernel(packed, rhs, forward, solved, matrix, right, upper, inverses):
    steps = matrix.shape[0] // BLK
    matrix[...] = jnp.zeros_like(matrix)
    for index, (i, j) in enumerate(blocks_of(steps)):
        matrix[i * BLK : (i + 1) * BLK, j * BLK : (j + 1) * BLK] = packed[index * BLK : (index + 1) * BLK, :]
    right[...] = rhs[...]
    solved[...] = jnp.zeros_like(solved)

    def eliminate(j, carry):
        here = pl.ds(pl.multiple_of(j * BLK, BLK), BLK)
        inverse = invert_factor(matrix[here, here])
        inverses[here, :] = inverse
        wide = dot(inverse, matrix[here, :])
        part = dot(inverse, right[here, :])
        cols = lax.broadcasted_iota(jnp.int32, wide.shape, 1)
        wide = jnp.where(cols >= (j + 1) * BLK, wide, 0.0)
        upper[here, :] = wide
        forward[here, :] = part
        matrix[...] -= dot(wide, wide, ((0,), (0,)))
        right[...] -= dot(wide, part, ((0,), (0,)))
        return carry

    lax.fori_loop(0, steps, eliminate, 0)

    def substitute(t, carry):
        here = pl.ds(pl.multiple_of((steps - 1 - t) * BLK, BLK), BLK)
        rest = forward[here, :] - dot(upper[here, :], solved[...])
        solved[here, :] = dot(inverses[here, :], rest, ((0,), (0,)))
        return carry

    lax.fori_loop(0, steps, substitute, 0)


def factor_and_solve(packed, rhs):
    size, width = rhs.shape
    out = jax.ShapeDtypeStruct((size, width), jnp.float32)
    return pl.pallas_call(
        solve_kernel,
        out_shape=(out, out),
        in_specs=[pl.BlockSpec(memory_space=pltpu.VMEM)] * 2,
        out_specs=[pl.BlockSpec(memory_space=pltpu.VMEM)] * 2,
        scratch_shapes=[
            pltpu.VMEM((size, size), jnp.float32),
            pltpu.VMEM((size, width), jnp.float32),
            pltpu.VMEM((size, size), jnp.float32),
            pltpu.VMEM((size, BLK), jnp.float32),
        ],
    )(packed, rhs)


def halves(x):
    high = x.astype(jnp.bfloat16)
    return high, (x - high.astype(jnp.float32)).astype(jnp.bfloat16)


def tail_kernel(
    mesh_sizes, row_block, solved, forward, panel, slack, scen_rhs, mask, border, rhs, reduced, directions,
    stage, high, low, held, split, total, landed, rhs_rows,
    stage_sem, rhs_sem, send_right, send_left, send_core, recv_right, recv_left, recv_core, scen_send, scen_recv,
):
    scen_count, col_count = mesh_sizes
    chips = col_count // 2
    scen = lax.axis_index("scen")
    col = lax.axis_index("col")
    chip, core = col // 2, col % 2
    sibling = chip * 2 + (1 - core)
    scen_local, pw, row_share = panel.shape
    pivot_width = pw // col_count
    own_width = border.shape[2]
    own_share = own_width // scen_count
    rhs_chunk = solved.shape[1] // CHUNKS
    units = scen_local * col_count
    chip_rows = 2 * scen_local * row_share

    def border_copy(unit):
        scenario, owner = unit // col_count, unit % col_count
        slot = unit % STAGES
        return pltpu.make_async_copy(
            border.at[scenario, pl.ds(pl.multiple_of(owner * row_share, row_share), row_share)],
            stage.at[slot],
            stage_sem.at[slot],
        )

    for unit in range(STAGES):
        border_copy(unit).start()
    rhs_copy = pltpu.make_async_copy(
        rhs.at[pl.ds(pl.multiple_of(scen * own_share, own_share), own_share)], rhs_rows, rhs_sem
    )
    rhs_copy.start()

    barrier = pltpu.get_barrier_semaphore()
    pl.semaphore_signal(barrier, inc=1, device_id={"col": sibling}, device_id_type=MESH)
    for d in range(1, scen_count):
        pl.semaphore_signal(
            barrier, inc=1, device_id={"scen": lax.rem(scen + d, scen_count)}, device_id_type=MESH
        )

    @pl.when(chip + 1 < chips)
    def _():
        pl.semaphore_signal(barrier, inc=1, device_id={"col": col + 2}, device_id_type=MESH)

    @pl.when(chip > 0)
    def _():
        pl.semaphore_signal(barrier, inc=1, device_id={"col": col - 2}, device_id_type=MESH)

    ends = jnp.where(chip + 1 < chips, 1, 0) + jnp.where(chip > 0, 1, 0)
    pl.semaphore_wait(barrier, scen_count + ends)

    def hop(q, origin, target, send, recv, lane=core):
        block = held.at[q, origin * 2 + lane]
        return pltpu.make_async_remote_copy(
            src_ref=block,
            dst_ref=block,
            send_sem=send.at[q, origin],
            recv_sem=recv.at[q, origin],
            device_id={"col": target},
            device_id_type=MESH,
        )

    def to_right(q, origin):
        return hop(q, origin, col + 2, send_right, recv_right)

    def to_left(q, origin):
        return hop(q, origin, col - 2, send_left, recv_left)

    def to_sibling(q, origin):
        return hop(q, origin, sibling, send_core, recv_core)

    def from_sibling(q, origin):
        return hop(q, origin, sibling, send_core, recv_core, 1 - core)

    def send_own(q):
        @pl.when(chip + 1 < chips)
        def _():
            to_right(q, chip).start()

        @pl.when(chip > 0)
        def _():
            to_left(q, chip).start()

        to_sibling(q, chip).start()

    def relay(q, distance):
        @pl.when(chip - distance >= 0)
        def _():
            origin = chip - distance
            to_right(q, origin).wait_recv()

            @pl.when(chip + 1 < chips)
            def _():
                to_right(q, origin).start()

            to_sibling(q, origin).start()

        @pl.when(chip + distance < chips)
        def _():
            origin = chip + distance
            to_left(q, origin).wait_recv()

            @pl.when(chip > 0)
            def _():
                to_left(q, origin).start()

            to_sibling(q, origin).start()

    def convert(begin, end):
        def body(unit, carry):
            scenario, owner = unit // col_count, unit % col_count
            slot = unit % STAGES
            place = ((owner // 2 * scen_local + scenario) * 2 + owner % 2) * row_share
            border_copy(unit).wait()
            for r in range(row_share // row_block):
                weight = mask[scenario, owner * (row_share // row_block) + r]

                def some(t, inner):
                    rows = r * row_block + t * 16
                    value = stage[slot, pl.ds(pl.multiple_of(rows, 16), 16), :] * weight
                    top = value.astype(jnp.bfloat16)
                    here = pl.ds(pl.multiple_of(place + rows, 16), 16)
                    high[here, :] = top
                    low[here, :] = (value - top.astype(jnp.float32)).astype(jnp.bfloat16)
                    return inner

                lax.fori_loop(0, row_block // 16, some, 0)

            @pl.when(unit + STAGES < units)
            def _():
                border_copy(unit + STAGES).start()

            return carry

        lax.fori_loop(begin, end, body, 0)

    own_slack = [
        slack[s, :, pl.ds(pl.multiple_of(col * row_share, row_share), row_share)] for s in range(scen_local)
    ]

    def own_rows(q):
        lanes = slice(q * rhs_chunk, (q + 1) * rhs_chunk)
        for s in range(scen_local):
            moved = dot(solved[:, lanes], panel[s], ((0,), (0,)))
            held[q, col, s] = moved / own_slack[s]
            directions[s, :, lanes] = moved.T

    def multiply(q, origin, first):
        for s in range(scen_local):
            for k in range(2):
                value = held[q, origin * 2 + k, s]
                top, rest = halves(value)
                lanes = slice((s * 2 + k) * row_share, (s * 2 + k + 1) * row_share)
                split[:rhs_chunk, lanes] = top
                split[rhs_chunk:, lanes] = rest
        width = min(512, own_width)
        rows = pl.ds(pl.multiple_of(origin * chip_rows, chip_rows), chip_rows)

        def body(n, carry):
            lanes = pl.ds(pl.multiple_of(n * width, width), width)
            both = jnp.dot(split[...], high[rows, lanes], preferred_element_type=jnp.float32)
            value = both[:rhs_chunk] + both[rhs_chunk:]
            value += jnp.dot(split[:rhs_chunk], low[rows, lanes], preferred_element_type=jnp.float32)
            if first:
                total[q, :, lanes] = value
            else:
                total[q, :, lanes] += value
            return carry

        lax.fori_loop(0, own_width // width, body, 0)

    def add_in(q, distance):
        if distance == 0:
            from_sibling(q, chip).wait_recv()
            multiply(q, chip, True)
            return

        @pl.when(chip - distance >= 0)
        def _():
            from_sibling(q, chip - distance).wait_recv()
            multiply(q, chip - distance, False)

        @pl.when(chip + distance < chips)
        def _():
            from_sibling(q, chip + distance).wait_recv()
            multiply(q, chip + distance, False)

    def share(q, d):
        peer = lax.rem(scen + d, scen_count)
        return pltpu.make_async_remote_copy(
            src_ref=total.at[q, :, pl.ds(pl.multiple_of(peer * own_share, own_share), own_share)],
            dst_ref=landed.at[q, d - 1],
            send_sem=scen_send.at[q, d - 1],
            recv_sem=scen_recv.at[q, d - 1],
            device_id={"scen": peer},
            device_id_type=MESH,
        )

    def finish(q):
        value = total[q, :, pl.ds(pl.multiple_of(scen * own_share, own_share), own_share)]
        for d in range(1, scen_count):
            share(q, d).wait_recv()
            value += landed[q, d - 1]
        lanes = slice(q * rhs_chunk, (q + 1) * rhs_chunk)
        reduced[:, lanes] = rhs_rows[:, lanes] - value.T

    own_rows(0)
    send_own(0)
    for q in range(1, CHUNKS):
        own_rows(q)
    steps = chips
    for t in range(steps):
        if t > 0:
            relay(0, t)
        convert(t * units // steps, (t + 1) * units // steps)
    rhs_copy.wait()
    for q in range(CHUNKS):
        for distance in range(chips):
            if q + 1 < CHUNKS:
                if distance == 0:
                    send_own(q + 1)
                else:
                    relay(q + 1, distance)
            add_in(q, distance)
        for d in range(1, scen_count):
            share(q, d).start()
        if q == 0:
            for s in range(scen_local):
                directions[s] = (scen_rhs[s] - directions[s]) / own_slack[s].T
        else:
            finish(q - 1)
    finish(CHUNKS - 1)

    @pl.when(scen == 0)
    def _():
        reduced[:pivot_width, :] = forward[pl.ds(pl.multiple_of(col * pivot_width, pivot_width), pivot_width), :]

    for q in range(CHUNKS):
        for origin in range(chips):
            @pl.when((origin <= chip) & (chip + 1 < chips))
            def _():
                to_right(q, origin).wait_send()

            @pl.when((origin >= chip) & (chip > 0))
            def _():
                to_left(q, origin).wait_send()

            to_sibling(q, origin).wait_send()
        for d in range(1, scen_count):
            share(q, d).wait_send()


def tail(solved, forward, panel, slack, scen_rhs, mask, border, rhs, row_block):
    scen_count = lax.axis_size("scen")
    col_count = lax.axis_size("col")
    chips = col_count // 2
    scen_local, _, row_share = panel.shape
    rhs_count = rhs.shape[1]
    _, row_total, own_width = border.shape
    own_share = own_width // scen_count
    rhs_chunk = rhs_count // CHUNKS
    vmem = pl.BlockSpec(memory_space=pltpu.VMEM)
    hbm = pl.BlockSpec(memory_space=pl.ANY)
    dma = pltpu.SemaphoreType.DMA
    return pl.pallas_call(
        functools.partial(tail_kernel, (scen_count, col_count), row_block),
        in_specs=[vmem] * 6 + [hbm] * 2,
        out_specs=[vmem] * 2,
        out_shape=(
            jax.ShapeDtypeStruct((own_share, rhs_count), jnp.float32),
            jax.ShapeDtypeStruct(scen_rhs.shape, jnp.float32),
        ),
        scratch_shapes=[
            pltpu.VMEM((STAGES, row_share, own_width), jnp.float32),
            pltpu.VMEM((scen_local * row_total, own_width), jnp.bfloat16),
            pltpu.VMEM((scen_local * row_total, own_width), jnp.bfloat16),
            pltpu.VMEM((CHUNKS, col_count, scen_local, rhs_chunk, row_share), jnp.float32),
            pltpu.VMEM((2 * rhs_chunk, 2 * scen_local * row_share), jnp.bfloat16),
            pltpu.VMEM((CHUNKS, rhs_chunk, own_width), jnp.float32),
            pltpu.VMEM((CHUNKS, scen_count - 1, rhs_chunk, own_share), jnp.float32),
            pltpu.VMEM((own_share, rhs_count), jnp.float32),
            dma((STAGES,)),
            dma,
        ]
        + [dma((CHUNKS, chips)) for _ in range(6)]
        + [dma((CHUNKS, scen_count - 1)) for _ in range(2)],
        compiler_params=pltpu.CompilerParams(
            collective_id=1, has_side_effects=True, vmem_limit_bytes=60 << 20
        ),
        cost_estimate=pl.CostEstimate(
            flops=6 * scen_local * row_total * own_width * rhs_count,
            bytes_accessed=4 * scen_local * row_total * own_width,
            transcendentals=0,
        ),
    )(solved, forward, panel, slack, scen_rhs, mask, border, rhs)


def per_device(border, pattern, slack, first_diag, rhs, scen_rhs):
    row_blocks, width_blocks = pattern.shape[1:]
    row_block = border.shape[1] // row_blocks
    col_block = border.shape[2] // width_blocks
    pivot_width = PW // lax.axis_size("col")
    mask = jnp.repeat(pattern.astype(jnp.float32), col_block, axis=2)[:, :, None, :]
    diagonal = jnp.tile(first_diag[:pivot_width], BLK // pivot_width)[None, :]
    slack = slack[:, None, :]
    panel, packed, rhs_panel = gather_panel(slack, mask, diagonal, border, rhs, row_block)
    forward, solved = factor_and_solve(packed, rhs_panel)
    reduced, directions = tail(solved, forward, panel, slack, scen_rhs, mask, border, rhs, row_block)
    return reduced[None], directions


def solution(mesh):
    return jax.shard_map(
        per_device,
        mesh=mesh,
        in_specs=(
            P("scen", None, "col"),
            P("scen", None, "col"),
            P("scen", None),
            P("col"),
            P("col", None),
            P("scen", "col", None),
        ),
        out_specs=(P("col", "scen", None), P("scen", "col", None)),
        check_vma=False,
    )
```

```python
import functools

import jax
import jax.numpy as jnp
from jax import lax
from jax.experimental import pallas as pl
from jax.experimental.pallas import tpu as pltpu
from jax.sharding import PartitionSpec as P

PW = 512
BLK = 128
HIGHEST = lax.Precision.HIGHEST
MESH = pl.DeviceIdType.MESH
CHUNKS = 2
STAGES = 4


def dot(a, b, contract=((1,), (0,))):
    return lax.dot_general(
        a, b, (contract, ((), ())), precision=HIGHEST, preferred_element_type=jnp.float32
    )


def halves(x):
    high = x.astype(jnp.bfloat16)
    return high, (x - high.astype(jnp.float32)).astype(jnp.bfloat16)


def blocks_of(steps):
    return [(i, j) for i in range(steps) for j in range(i, steps)]


def invert_factor(block):
    groups = BLK // 8
    shape = (8, BLK)
    sub = lax.broadcasted_iota(jnp.int32, shape, 0)
    lane = lax.broadcasted_iota(jnp.int32, shape, 1)
    rows = [block[8 * i : 8 * i + 8, :] for i in range(groups)]
    inverse = [jnp.where(lane == sub + 8 * i, 1.0, 0.0).astype(jnp.float32) for i in range(groups)]
    for g in range(groups):
        columns = [
            {i: jnp.broadcast_to(rows[i][:, 8 * g + m : 8 * g + m + 1], shape) for i in range(g, groups)}
            for m in range(8)
        ]
        pivots = jnp.ones(shape, jnp.float32)
        for m in range(8):
            head = columns[m][g]
            pivot = jnp.broadcast_to(head[m : m + 1, :], shape)
            scale = 1.0 / pivot
            pivots = jnp.where(sub == m, pivot, pivots)
            row = jnp.broadcast_to(rows[g][m : m + 1, :], shape) * scale
            inverse_row = jnp.broadcast_to(inverse[g][m : m + 1, :], shape) * scale
            factors = [
                jnp.broadcast_to(head[later : later + 1, :], shape) * scale for later in range(m + 1, 8)
            ]
            for i in range(g, groups):
                column = columns[m][i]
                if i == g:
                    column = jnp.where(sub > m, column, 0.0)
                rows[i] = rows[i] - column * row
                inverse[i] = inverse[i] - column * inverse_row
                for later in range(m + 1, 8):
                    columns[later][i] = columns[later][i] - column * factors[later - m - 1]
        inverse[g] = inverse[g] * lax.rsqrt(pivots)
    return jnp.concatenate(inverse, axis=0)


def factor_and_solve(matrix, right, forward, solved, upper, inverses):
    steps = matrix.shape[0] // BLK
    solved[...] = jnp.zeros_like(solved)

    def eliminate(j, carry):
        here = pl.ds(pl.multiple_of(j * BLK, BLK), BLK)
        inverse = invert_factor(matrix[here, here])
        inverses[here, :] = inverse
        wide = dot(inverse, matrix[here, :])
        part = dot(inverse, right[here, :])
        cols = lax.broadcasted_iota(jnp.int32, wide.shape, 1)
        wide = jnp.where(cols >= (j + 1) * BLK, wide, 0.0)
        upper[here, :] = wide
        forward[here, :] = part
        matrix[...] -= dot(wide, wide, ((0,), (0,)))
        right[...] -= dot(wide, part, ((0,), (0,)))
        return carry

    lax.fori_loop(0, steps, eliminate, 0)

    def substitute(t, carry):
        here = pl.ds(pl.multiple_of((steps - 1 - t) * BLK, BLK), BLK)
        rest = forward[here, :] - dot(upper[here, :], solved[...])
        solved[here, :] = dot(inverses[here, :], rest, ((0,), (0,)))
        return carry

    lax.fori_loop(0, steps, substitute, 0)


def whole_kernel(
    mesh_sizes, row_block, slack, mask, diagonal, scen_rhs, border, rhs, reduced, directions,
    panel, packed, rhs_panel, raw, sent, gram, pair, pieces, matrix, upper, inverses, forward, solved,
    stage, high, low, held, split, total, landed, rhs_rows,
    raw_sem, rhs_sem, out_send, out_recv, rhs_send, rhs_recv, rhs_core_send, rhs_core_recv,
    pair_sems, sum_send, sum_recv, all_send, all_recv, core_sems,
    stage_sem, own_rhs_sem, send_right, send_left, send_core, recv_right, recv_left, recv_core,
    scen_send, scen_recv,
):
    scen_count, col_count = mesh_sizes
    chips = col_count // 2
    places = scen_count * chips
    scen = lax.axis_index("scen")
    col = lax.axis_index("col")
    chip, core = col // 2, col % 2
    sibling = chip * 2 + (1 - core)
    place = scen * chips + chip
    scen_local, pw, row_share = panel.shape
    pivot_width = pw // col_count
    lanes_read = raw.shape[3]
    piece = pieces.shape[1]
    half = piece * places

    def target(t):
        return lax.rem(col + col_count // 2 + t, col_count)

    def rows_of(owner):
        return pl.ds(pl.multiple_of(owner * row_share, row_share), row_share)

    def pivots_of(owner):
        return pl.ds(pl.multiple_of(owner * pivot_width, pivot_width), pivot_width)

    def read(t):
        return pltpu.make_async_copy(
            border.at[:, rows_of(target(t)), pl.ds(0, lanes_read)], raw.at[t], raw_sem.at[t]
        )

    for t in range(col_count):
        read(t).start()
    own_rhs = pltpu.make_async_copy(rhs.at[pl.ds(0, pivot_width)], rhs_panel.at[pivots_of(col)], rhs_sem)
    own_rhs.start()

    own_width = border.shape[2]
    own_share = own_width // scen_count
    rhs_chunk = rhs.shape[1] // CHUNKS
    blocks = border.shape[1] // row_block
    units = scen_local * blocks
    chip_rows = 2 * scen_local * row_share

    def border_copy(unit):
        scenario, block = unit // blocks, unit % blocks
        slot = unit % STAGES
        return pltpu.make_async_copy(
            border.at[scenario, pl.ds(pl.multiple_of(block * row_block, row_block), row_block)],
            stage.at[slot],
            stage_sem.at[slot],
        )

    for unit in range(STAGES):
        border_copy(unit).start()
    rhs_copy = pltpu.make_async_copy(
        rhs.at[pl.ds(pl.multiple_of(scen * own_share, own_share), own_share)], rhs_rows, own_rhs_sem
    )
    rhs_copy.start()

    def convert(begin, end):
        def body(unit, carry):
            scenario, block = unit // blocks, unit % blocks
            slot = unit % STAGES
            owner = block * row_block // row_share
            place = (owner // 2 * scen_local + scenario) * 2 + owner % 2
            base = place * row_share + block * row_block % row_share
            border_copy(unit).wait()
            weight = mask[scenario, block]

            def some(t, inner):
                value = stage[slot, pl.ds(pl.multiple_of(t * 16, 16), 16), :] * weight
                top = value.astype(jnp.bfloat16)
                here = pl.ds(pl.multiple_of(base + t * 16, 16), 16)
                high[here, :] = top
                low[here, :] = (value - top.astype(jnp.float32)).astype(jnp.bfloat16)
                return inner

            lax.fori_loop(0, row_block // 16, some, 0)

            @pl.when(unit + STAGES < units)
            def _():
                border_copy(unit + STAGES).start()

            return carry

        lax.fori_loop(begin, end, body, 0)

    barrier = pltpu.get_barrier_semaphore()

    def greet(device):
        pl.semaphore_signal(barrier, inc=1, device_id=device, device_id_type=MESH)

    def away(e):
        other = lax.rem(place + e, places)
        return {"scen": other // chips, "col": lax.rem(other, chips) * 2 + core}

    def across(e):
        return {"col": lax.rem(chip + e, chips) * 2 + (1 - core)}

    for e in range(1, places):
        greet(away(e))
    for e in range(chips):
        greet(across(e))

    def hand_out(t):
        return pltpu.make_async_remote_copy(
            src_ref=sent.at[t],
            dst_ref=panel.at[:, pivots_of(col), :],
            send_sem=out_send.at[t],
            recv_sem=out_recv.at[t],
            device_id={"col": target(t)},
            device_id_type=MESH,
        )

    def hand_in(t):
        source = lax.rem(col + 2 * col_count - col_count // 2 - t, col_count)
        return pltpu.make_async_remote_copy(
            src_ref=sent.at[t],
            dst_ref=panel.at[:, pivots_of(source), :],
            send_sem=out_send.at[t],
            recv_sem=out_recv.at[t],
            device_id={"col": source},
            device_id_type=MESH,
        )

    here = col_count - col_count // 2
    for t in range(col_count):
        read(t).wait()
        for s in range(scen_local):
            for r in range(row_share // row_block):
                weight = mask[s, target(t) * (row_share // row_block) + r, :, :lanes_read]
                value = raw[t, s, r * row_block : (r + 1) * row_block, :] * weight
                value = value.T[:pivot_width]
                if t == here:
                    panel[s, pivots_of(col), r * row_block : (r + 1) * row_block] = value
                else:
                    sent[t, s, :, r * row_block : (r + 1) * row_block] = value
        if t == 0:
            pl.semaphore_wait(barrier, places - 1 + chips)
        if t != here:
            hand_out(t).start()

    def rhs_away(e, origin_shift=0):
        return pltpu.make_async_remote_copy(
            src_ref=rhs_panel.at[pivots_of(col)],
            dst_ref=rhs_panel.at[pivots_of(col)],
            send_sem=rhs_send.at[e - 1],
            recv_sem=rhs_recv.at[e - 1],
            device_id={"col": lax.rem(chip + e, chips) * 2 + core},
            device_id_type=MESH,
        )

    def rhs_from(e):
        source = lax.rem(chip + chips - e, chips) * 2 + core
        return pltpu.make_async_remote_copy(
            src_ref=rhs_panel.at[pivots_of(source)],
            dst_ref=rhs_panel.at[pivots_of(source)],
            send_sem=rhs_send.at[e - 1],
            recv_sem=rhs_recv.at[e - 1],
            device_id={"col": source},
            device_id_type=MESH,
        )

    def rhs_core(e, side):
        owner = lax.rem(chip + chips - e, chips) * 2 + side
        return pltpu.make_async_remote_copy(
            src_ref=rhs_panel.at[pivots_of(owner)],
            dst_ref=rhs_panel.at[pivots_of(owner)],
            send_sem=rhs_core_send.at[e],
            recv_sem=rhs_core_recv.at[e],
            device_id={"col": sibling},
            device_id_type=MESH,
        )

    convert(0, units)
    for t in range(col_count):
        if t != here:
            hand_in(t).wait_recv()

    own_rhs.wait()
    for e in range(1, chips):
        rhs_away(e).start()
    rhs_core(0, core).start()

    steps = pw // BLK
    whole = [panel[s] for s in range(scen_local)]
    scaled = [panel[s] / slack[s, :, rows_of(col)] for s in range(scen_local)]
    whole = jnp.concatenate(whole, axis=1)
    scaled = jnp.concatenate(scaled, axis=1)
    row = lax.broadcasted_iota(jnp.int32, (BLK, BLK), 0)
    lane = lax.broadcasted_iota(jnp.int32, (BLK, BLK), 1)
    index = 0
    for i in range(steps):
        wide = dot(scaled[i * BLK : (i + 1) * BLK], whole[i * BLK :], ((1,), (1,)))
        mine = (row == lane) & ((lane + i * BLK) // pivot_width == col) & (scen == 0)
        for j in range(i, steps):
            value = wide[:, (j - i) * BLK : (j - i + 1) * BLK]
            if i == j:
                value = value + jnp.where(mine, jnp.broadcast_to(diagonal[...], (BLK, BLK)), 0.0)
            gram[index * BLK : (index + 1) * BLK, :] = value
            index += 1
    if index * BLK < gram.shape[0]:
        gram[index * BLK :, :] = jnp.zeros((gram.shape[0] - index * BLK, BLK), jnp.float32)

    def half_of(side):
        return pl.ds(pl.multiple_of(side * half, 8), half)

    swap = pltpu.make_async_remote_copy(
        src_ref=gram.at[half_of(1 - core)],
        dst_ref=pair,
        send_sem=pair_sems.at[0],
        recv_sem=pair_sems.at[1],
        device_id={"col": sibling},
        device_id_type=MESH,
    )
    swap.start()
    swap.wait_recv()
    pair[...] += gram[half_of(core), :]

    def piece_of(index):
        return pl.ds(pl.multiple_of(index * piece, 8), piece)

    def spread(e):
        return pltpu.make_async_remote_copy(
            src_ref=pair.at[piece_of(lax.rem(place + e, places))],
            dst_ref=pieces.at[e - 1],
            send_sem=sum_send.at[e - 1],
            recv_sem=sum_recv.at[e - 1],
            device_id=away(e),
            device_id_type=MESH,
        )

    for e in range(1, places):
        spread(e).start()
    for e in range(1, chips):
        rhs_from(e).wait_recv()
        rhs_core(e, core).start()
    value = pair[piece_of(place), :]
    for e in range(1, places):
        spread(e).wait_recv()
        value += pieces[e - 1]

    def slot_of(index):
        return pl.ds(pl.multiple_of(core * half + index * piece, 8), piece)

    packed[slot_of(place), :] = value

    def collect(e, origin):
        return pltpu.make_async_remote_copy(
            src_ref=packed.at[slot_of(origin)],
            dst_ref=packed.at[slot_of(origin)],
            send_sem=all_send.at[e - 1],
            recv_sem=all_recv.at[e - 1],
            device_id=away(e),
            device_id_type=MESH,
        )

    for e in range(1, places):
        collect(e, place).start()
    for e in range(1, places):
        collect(e, lax.rem(place + places - e, places)).wait_recv()

    def finish(side):
        return pltpu.make_async_remote_copy(
            src_ref=packed.at[half_of(side)],
            dst_ref=packed.at[half_of(side)],
            send_sem=core_sems.at[0],
            recv_sem=core_sems.at[1],
            device_id={"col": sibling},
            device_id_type=MESH,
        )

    finish(core).start()
    for e in range(chips):
        rhs_core(e, 1 - core).wait_recv()
    finish(1 - core).wait_recv()
    for t in range(col_count):
        if t != here:
            hand_out(t).wait_send()
    for e in range(1, chips):
        rhs_away(e).wait_send()
    for e in range(chips):
        rhs_core(e, core).wait_send()
    swap.wait_send()
    for e in range(1, places):
        spread(e).wait_send()
        collect(e, place).wait_send()
    finish(core).wait_send()

    matrix[...] = jnp.zeros_like(matrix)
    for index, (i, j) in enumerate(blocks_of(steps)):
        matrix[i * BLK : (i + 1) * BLK, j * BLK : (j + 1) * BLK] = packed[index * BLK : (index + 1) * BLK, :]
    factor_and_solve(matrix, rhs_panel, forward, solved, upper, inverses)

    own_slack = [slack[s, :, rows_of(col)] for s in range(scen_local)]

    def hop(q, origin, target, send, recv, lane=core):
        block = held.at[q, origin * 2 + lane]
        return pltpu.make_async_remote_copy(
            src_ref=block,
            dst_ref=block,
            send_sem=send,
            recv_sem=recv.at[q, origin],
            device_id={"col": target},
            device_id_type=MESH,
        )

    def to_right(q, origin, d=1):
        return hop(q, origin, col + 2 * d, send_right.at[q, origin, d - 1], recv_right)

    def to_left(q, origin, d=1):
        return hop(q, origin, col - 2 * d, send_left.at[q, origin, d - 1], recv_left)

    def to_sibling(q, origin):
        return hop(q, origin, sibling, send_core.at[q, origin], recv_core)

    def from_sibling(q, origin):
        return hop(q, origin, sibling, send_core.at[q, origin], recv_core, 1 - core)

    def send_own(q):
        for d in (1, 2):
            @pl.when(chip + d < chips)
            def _():
                to_right(q, chip, d).start()

            @pl.when(chip >= d)
            def _():
                to_left(q, chip, d).start()

        to_sibling(q, chip).start()

    def arrive(q, distance):
        @pl.when(chip >= distance)
        def _():
            origin = chip - distance
            to_right(q, origin).wait_recv()
            if distance >= 2:
                @pl.when(chip + 1 < chips)
                def _():
                    to_right(q, origin).start()

            to_sibling(q, origin).start()

        @pl.when(chip + distance < chips)
        def _():
            origin = chip + distance
            to_left(q, origin).wait_recv()
            if distance >= 2:
                @pl.when(chip > 0)
                def _():
                    to_left(q, origin).start()

            to_sibling(q, origin).start()

    def own_rows(q):
        lanes = slice(q * rhs_chunk, (q + 1) * rhs_chunk)
        for s in range(scen_local):
            moved = dot(solved[:, lanes], panel[s], ((0,), (0,)))
            held[q, col, s] = moved / own_slack[s]
            directions[s, :, lanes] = moved.T

    def multiply(q, origin, first):
        for s in range(scen_local):
            for k in range(2):
                top, rest = halves(held[q, origin * 2 + k, s])
                lanes = slice((s * 2 + k) * row_share, (s * 2 + k + 1) * row_share)
                split[:rhs_chunk, lanes] = top
                split[rhs_chunk:, lanes] = rest
        width = min(512, own_width)
        rows = pl.ds(pl.multiple_of(origin * chip_rows, chip_rows), chip_rows)

        def body(n, carry):
            lanes = pl.ds(pl.multiple_of(n * width, width), width)
            both = jnp.dot(split[...], high[rows, lanes], preferred_element_type=jnp.float32)
            value = both[:rhs_chunk] + both[rhs_chunk:]
            value += jnp.dot(split[:rhs_chunk], low[rows, lanes], preferred_element_type=jnp.float32)
            if first:
                total[q, :, lanes] = value
            else:
                total[q, :, lanes] += value
            return carry

        lax.fori_loop(0, own_width // width, body, 0)

    def add_in(q, distance):
        if distance == 0:
            from_sibling(q, chip).wait_recv()
            multiply(q, chip, True)
            return

        @pl.when(chip >= distance)
        def _():
            from_sibling(q, chip - distance).wait_recv()
            multiply(q, chip - distance, False)

        @pl.when(chip + distance < chips)
        def _():
            from_sibling(q, chip + distance).wait_recv()
            multiply(q, chip + distance, False)

    def share(q, d):
        peer = lax.rem(scen + d, scen_count)
        return pltpu.make_async_remote_copy(
            src_ref=total.at[q, :, pl.ds(pl.multiple_of(peer * own_share, own_share), own_share)],
            dst_ref=landed.at[q, d - 1],
            send_sem=scen_send.at[q, d - 1],
            recv_sem=scen_recv.at[q, d - 1],
            device_id={"scen": peer},
            device_id_type=MESH,
        )

    def finish_chunk(q):
        value = total[q, :, pl.ds(pl.multiple_of(scen * own_share, own_share), own_share)]
        for d in range(1, scen_count):
            share(q, d).wait_recv()
            value += landed[q, d - 1]
        lanes = slice(q * rhs_chunk, (q + 1) * rhs_chunk)
        reduced[:, lanes] = rhs_rows[:, lanes] - value.T

    own_rows(0)
    send_own(0)
    for q in range(1, CHUNKS):
        own_rows(q)
    rhs_copy.wait()
    for q in range(CHUNKS):
        for distance in range(chips):
            if distance + 1 < chips:
                arrive(q, distance + 1)
            if distance == 0 and q + 1 < CHUNKS:
                send_own(q + 1)
            add_in(q, distance)
        for d in range(1, scen_count):
            share(q, d).start()
        if q == 0:
            for s in range(scen_local):
                directions[s] = (scen_rhs[s] - directions[s]) / own_slack[s].T
        else:
            finish_chunk(q - 1)
    finish_chunk(CHUNKS - 1)

    @pl.when(scen == 0)
    def _():
        reduced[:pivot_width, :] = forward[pivots_of(col), :]

    for q in range(CHUNKS):
        for d in (1, 2):
            @pl.when(chip + d < chips)
            def _():
                to_right(q, chip, d).wait_send()

            @pl.when(chip >= d)
            def _():
                to_left(q, chip, d).wait_send()

        for distance in range(2, chips):
            @pl.when((chip >= distance) & (chip + 1 < chips))
            def _():
                to_right(q, chip - distance).wait_send()

            @pl.when((chip + distance < chips) & (chip > 0))
            def _():
                to_left(q, chip + distance).wait_send()

        for origin in range(chips):
            to_sibling(q, origin).wait_send()
        for d in range(1, scen_count):
            share(q, d).wait_send()


def eliminate_panel(slack, mask, diagonal, scen_rhs, border, rhs, row_block):
    scen_count = lax.axis_size("scen")
    col_count = lax.axis_size("col")
    chips = col_count // 2
    places = scen_count * chips
    scen_local, row_total, own_width = border.shape
    row_share = row_total // col_count
    own_share = own_width // scen_count
    pivot_width = PW // col_count
    rhs_count = rhs.shape[1]
    rhs_chunk = rhs_count // CHUNKS
    lanes_read = -(-pivot_width // BLK) * BLK
    count = len(blocks_of(PW // BLK)) * BLK
    piece = -(-count // (2 * places * 8)) * 8
    half = piece * places
    vmem = pl.BlockSpec(memory_space=pltpu.VMEM)
    hbm = pl.BlockSpec(memory_space=pl.ANY)
    dma = pltpu.SemaphoreType.DMA

    def floats(*shape):
        return pltpu.VMEM(shape, jnp.float32)

    return pl.pallas_call(
        functools.partial(whole_kernel, (scen_count, col_count), row_block),
        in_specs=[vmem] * 4 + [hbm] * 2,
        out_specs=[vmem] * 2,
        out_shape=(
            jax.ShapeDtypeStruct((own_share, rhs_count), jnp.float32),
            jax.ShapeDtypeStruct(scen_rhs.shape, jnp.float32),
        ),
        scratch_shapes=[
            floats(scen_local, PW, row_share),
            floats(2 * half, BLK),
            floats(PW, rhs_count),
            floats(col_count, scen_local, row_share, lanes_read),
            floats(col_count, scen_local, pivot_width, row_share),
            floats(2 * half, BLK),
            floats(half, BLK),
            floats(places - 1, piece, BLK),
            floats(PW, PW),
            floats(PW, PW),
            floats(PW, BLK),
            floats(PW, rhs_count),
            floats(PW, rhs_count),
            floats(STAGES, row_block, own_width),
            pltpu.VMEM((scen_local * row_total, own_width), jnp.bfloat16),
            pltpu.VMEM((scen_local * row_total, own_width), jnp.bfloat16),
            floats(CHUNKS, col_count, scen_local, rhs_chunk, row_share),
            pltpu.VMEM((2 * rhs_chunk, 2 * scen_local * row_share), jnp.bfloat16),
            floats(CHUNKS, rhs_chunk, own_width),
            floats(CHUNKS, scen_count - 1, rhs_chunk, own_share),
            floats(own_share, rhs_count),
            dma((col_count,)),
            dma,
            dma((col_count,)),
            dma((col_count,)),
            dma((chips - 1,)),
            dma((chips - 1,)),
            dma((chips,)),
            dma((chips,)),
            dma((2,)),
            dma((places - 1,)),
            dma((places - 1,)),
            dma((places - 1,)),
            dma((places - 1,)),
            dma((2,)),
            dma((STAGES,)),
            dma,
            dma((CHUNKS, chips, 2)),
            dma((CHUNKS, chips, 2)),
            dma((CHUNKS, chips)),
            dma((CHUNKS, chips)),
            dma((CHUNKS, chips)),
            dma((CHUNKS, chips)),
            dma((CHUNKS, scen_count - 1)),
            dma((CHUNKS, scen_count - 1)),
        ],
        compiler_params=pltpu.CompilerParams(
            collective_id=0, has_side_effects=True, vmem_limit_bytes=63 << 20
        ),
        cost_estimate=pl.CostEstimate(
            flops=6 * scen_local * row_total * own_width * rhs_count,
            bytes_accessed=4 * scen_local * row_total * own_width,
            transcendentals=0,
        ),
    )(slack, mask, diagonal, scen_rhs, border, rhs)


def per_device(border, pattern, slack, first_diag, rhs, scen_rhs):
    row_blocks, width_blocks = pattern.shape[1:]
    row_block = border.shape[1] // row_blocks
    col_block = border.shape[2] // width_blocks
    pivot_width = PW // lax.axis_size("col")
    mask = jnp.repeat(pattern.astype(jnp.float32), col_block, axis=2)[:, :, None, :]
    diagonal = jnp.tile(first_diag[:pivot_width], BLK // pivot_width)[None, :]
    reduced, directions = eliminate_panel(
        slack[:, None, :], mask, diagonal, scen_rhs, border, rhs, row_block
    )
    return reduced[None], directions


def solution(mesh):
    return jax.shard_map(
        per_device,
        mesh=mesh,
        in_specs=(
            P("scen", None, "col"),
            P("scen", None, "col"),
            P("scen", None),
            P("col"),
            P("col", None),
            P("scen", "col", None),
        ),
        out_specs=(P("col", "scen", None), P("scen", "col", None)),
        check_vma=False,
    )
```

```python
import functools

import jax
import jax.numpy as jnp
from jax import lax
from jax.experimental import pallas as pl
from jax.experimental.pallas import tpu as pltpu
from jax.sharding import PartitionSpec as P

PW = 512
BLK = 128
HIGHEST = lax.Precision.HIGHEST
MESH = pl.DeviceIdType.MESH
CHUNKS = (2, 4, 4)
STAGES = 2


def dot(a, b, contract=((1,), (0,))):
    return lax.dot_general(
        a, b, (contract, ((), ())), precision=HIGHEST, preferred_element_type=jnp.float32
    )


def halves(x):
    high = x.astype(jnp.bfloat16)
    return high, (x - high.astype(jnp.float32)).astype(jnp.bfloat16)


def blocks_of(steps):
    return [(i, j) for i in range(steps) for j in range(i, steps)]


def invert_factor(block):
    groups = BLK // 8
    shape = (8, BLK)
    sub = lax.broadcasted_iota(jnp.int32, shape, 0)
    lane = lax.broadcasted_iota(jnp.int32, shape, 1)
    rows = [block[8 * i : 8 * i + 8, :] for i in range(groups)]
    inverse = [jnp.where(lane == sub + 8 * i, 1.0, 0.0).astype(jnp.float32) for i in range(groups)]
    for g in range(groups):
        columns = [
            {i: jnp.broadcast_to(rows[i][:, 8 * g + m : 8 * g + m + 1], shape) for i in range(g, groups)}
            for m in range(8)
        ]
        pivots = jnp.ones(shape, jnp.float32)
        for m in range(8):
            head = columns[m][g]
            pivot = jnp.broadcast_to(head[m : m + 1, :], shape)
            scale = 1.0 / pivot
            pivots = jnp.where(sub == m, pivot, pivots)
            row = jnp.broadcast_to(rows[g][m : m + 1, :], shape) * scale
            inverse_row = jnp.broadcast_to(inverse[g][m : m + 1, :], shape) * scale
            factors = [
                jnp.broadcast_to(head[later : later + 1, :], shape) * scale for later in range(m + 1, 8)
            ]
            for i in range(g, groups):
                column = columns[m][i]
                if i == g:
                    column = jnp.where(sub > m, column, 0.0)
                rows[i] = rows[i] - column * row
                inverse[i] = inverse[i] - column * inverse_row
                for later in range(m + 1, 8):
                    columns[later][i] = columns[later][i] - column * factors[later - m - 1]
        inverse[g] = inverse[g] * lax.rsqrt(pivots)
    return jnp.concatenate(inverse, axis=0)


def factor_and_solve(matrix, right, forward, solved, upper, inverses, between):
    steps = matrix.shape[0] // BLK

    def block(i):
        return slice(i * BLK, (i + 1) * BLK)

    def eliminate(j, carry):
        here = pl.ds(pl.multiple_of(j * BLK, BLK), BLK)
        inverse = invert_factor(matrix[here, here])
        inverses[here, :] = inverse
        forward[here, :] = dot(inverse, right[here, :])
        for now in range(steps - 1):
            @pl.when(j == now)
            def _():
                wide = dot(inverse, matrix[block(now), (now + 1) * BLK :])
                upper[block(now), (now + 1) * BLK :] = wide
                for i in range(now + 1, steps):
                    rows = wide[:, (i - now - 1) * BLK : (i - now) * BLK]
                    matrix[block(i), i * BLK :] -= dot(rows, wide[:, (i - now - 1) * BLK :], ((0,), (0,)))
                right[(now + 1) * BLK :, :] -= dot(wide, forward[block(now), :], ((0,), (0,)))
                between(now)
        return carry

    lax.fori_loop(0, steps, eliminate, 0)
    for j in reversed(range(steps)):
        rest = forward[block(j), :]
        if j + 1 < steps:
            rest = rest - dot(upper[block(j), (j + 1) * BLK :], solved[(j + 1) * BLK :, :])
        solved[block(j), :] = dot(inverses[block(j), :], rest, ((0,), (0,)))


def whole_kernel(
    mesh_sizes, slack, pattern, diagonal, scen_rhs, border, rhs, reduced, directions,
    panel, packed, rhs_panel, raw, sent, gram, pair, pieces, matrix, upper, inverses, forward, solved,
    mask, early, stage, high, low, held, split, total, landed, rhs_rows,
    raw_sem, rhs_sem, out_send, out_recv, rhs_send, rhs_recv, rhs_core_send, rhs_core_recv,
    pair_sems, sum_send, sum_recv, all_send, all_recv, core_sems,
    stage_sem, own_rhs_sem, send_right, send_left, send_core, recv_right, recv_left, recv_core,
    scen_send, scen_recv,
):
    scen_count, col_count = mesh_sizes
    chips = col_count // 2
    places = scen_count * chips
    scen = lax.axis_index("scen")
    col = lax.axis_index("col")
    chip, core = col // 2, col % 2
    sibling = chip * 2 + (1 - core)
    place = scen * chips + chip
    scen_local, pw, row_share = panel.shape
    row_blocks, width_blocks = pattern.shape[1:]
    row_block = border.shape[1] // row_blocks
    col_block = border.shape[2] // width_blocks
    pivot_width = pw // col_count
    lanes_read = raw.shape[3]
    piece = pieces.shape[1]
    half = piece * places

    def target(t):
        return lax.rem(col + col_count // 2 + t, col_count)

    def rows_of(owner):
        return pl.ds(pl.multiple_of(owner * row_share, row_share), row_share)

    def pivots_of(owner):
        return pl.ds(pl.multiple_of(owner * pivot_width, pivot_width), pivot_width)

    def read(t):
        return pltpu.make_async_copy(
            border.at[:, rows_of(target(t)), pl.ds(0, lanes_read)], raw.at[t], raw_sem.at[t]
        )

    for t in range(col_count):
        read(t).start()
    own_rhs = pltpu.make_async_copy(rhs.at[pl.ds(0, pivot_width)], rhs_panel.at[pivots_of(col)], rhs_sem)
    own_rhs.start()

    own_width = border.shape[2]
    own_share = own_width // scen_count
    bounds = chunk_bounds(rhs.shape[1])
    pieces_per_row = row_share // BLK
    parts = scen_local * pieces_per_row
    blocks = border.shape[1] // row_block
    units = scen_local * blocks
    chip_rows = 2 * scen_local * row_share

    def border_copy(unit):
        scenario, block = unit // blocks, unit % blocks
        slot = unit % STAGES
        return pltpu.make_async_copy(
            border.at[scenario, pl.ds(pl.multiple_of(block * row_block, row_block), row_block)],
            stage.at[slot],
            stage_sem.at[slot],
        )

    for unit in range(STAGES):
        border_copy(unit).start()
    rhs_copy = pltpu.make_async_copy(
        rhs.at[pl.ds(pl.multiple_of(scen * own_share, own_share), own_share)], rhs_rows, own_rhs_sem
    )
    rhs_copy.start()

    def convert(begin, end):
        def body(unit, carry):
            scenario, block = unit // blocks, unit % blocks
            slot = unit % STAGES
            owner = block * row_block // row_share
            place = (owner // 2 * scen_local + scenario) * 2 + owner % 2
            base = place * row_share + block * row_block % row_share
            border_copy(unit).wait()
            weight = mask[scenario, block]

            def some(t, inner):
                value = stage[slot, pl.ds(pl.multiple_of(t * 16, 16), 16), :] * weight
                top = value.astype(jnp.bfloat16)
                here = pl.ds(pl.multiple_of(base + t * 16, 16), 16)
                high[here, :] = top
                low[here, :] = (value - top.astype(jnp.float32)).astype(jnp.bfloat16)
                return inner

            lax.fori_loop(0, row_block // 16, some, 0)

            @pl.when(unit + STAGES < units)
            def _():
                border_copy(unit + STAGES).start()

            return carry

        lax.fori_loop(begin, end, body, 0)

    barrier = pltpu.get_barrier_semaphore()

    def greet(device):
        pl.semaphore_signal(barrier, inc=1, device_id=device, device_id_type=MESH)

    def away(e):
        other = lax.rem(place + e, places)
        return {"scen": other // chips, "col": lax.rem(other, chips) * 2 + core}

    def across(e):
        return {"col": lax.rem(chip + e, chips) * 2 + (1 - core)}

    for e in range(1, places):
        greet(away(e))
    for e in range(chips):
        greet(across(e))

    for s in range(scen_local):
        ones = pattern[s].astype(jnp.float32)
        wide = [jnp.broadcast_to(ones[:, c : c + 1], (row_blocks, col_block)) for c in range(width_blocks)]
        wide = jnp.concatenate(wide, axis=1)
        for r in range(row_blocks):
            mask[s, r] = wide[r : r + 1]

    def hand_out(t):
        return pltpu.make_async_remote_copy(
            src_ref=sent.at[t],
            dst_ref=panel.at[:, pivots_of(col), :],
            send_sem=out_send.at[t],
            recv_sem=out_recv.at[t],
            device_id={"col": target(t)},
            device_id_type=MESH,
        )

    def hand_in(t):
        source = lax.rem(col + 2 * col_count - col_count // 2 - t, col_count)
        return pltpu.make_async_remote_copy(
            src_ref=sent.at[t],
            dst_ref=panel.at[:, pivots_of(source), :],
            send_sem=out_send.at[t],
            recv_sem=out_recv.at[t],
            device_id={"col": source},
            device_id_type=MESH,
        )

    here = col_count - col_count // 2
    for t in range(col_count):
        read(t).wait()
        for s in range(scen_local):
            for r in range(row_share // row_block):
                weight = mask[s, target(t) * (row_share // row_block) + r, :, :lanes_read]
                value = raw[t, s, r * row_block : (r + 1) * row_block, :] * weight
                value = value.T[:pivot_width]
                if t == here:
                    panel[s, pivots_of(col), r * row_block : (r + 1) * row_block] = value
                else:
                    sent[t, s, :, r * row_block : (r + 1) * row_block] = value
        if t == 0:
            pl.semaphore_wait(barrier, places - 1 + chips)
        if t != here:
            hand_out(t).start()

    def rhs_away(e, origin_shift=0):
        return pltpu.make_async_remote_copy(
            src_ref=rhs_panel.at[pivots_of(col)],
            dst_ref=rhs_panel.at[pivots_of(col)],
            send_sem=rhs_send.at[e - 1],
            recv_sem=rhs_recv.at[e - 1],
            device_id={"col": lax.rem(chip + e, chips) * 2 + core},
            device_id_type=MESH,
        )

    def rhs_from(e):
        source = lax.rem(chip + chips - e, chips) * 2 + core
        return pltpu.make_async_remote_copy(
            src_ref=rhs_panel.at[pivots_of(source)],
            dst_ref=rhs_panel.at[pivots_of(source)],
            send_sem=rhs_send.at[e - 1],
            recv_sem=rhs_recv.at[e - 1],
            device_id={"col": source},
            device_id_type=MESH,
        )

    def rhs_core(e, side):
        owner = lax.rem(chip + chips - e, chips) * 2 + side
        return pltpu.make_async_remote_copy(
            src_ref=rhs_panel.at[pivots_of(owner)],
            dst_ref=rhs_panel.at[pivots_of(owner)],
            send_sem=rhs_core_send.at[e],
            recv_sem=rhs_core_recv.at[e],
            device_id={"col": sibling},
            device_id_type=MESH,
        )

    convert(0, units)
    for t in range(col_count):
        if t != here:
            hand_in(t).wait_recv()

    own_rhs.wait()
    for e in range(1, chips):
        rhs_away(e).start()
    rhs_core(0, core).start()

    steps = pw // BLK
    whole = [panel[s] for s in range(scen_local)]
    scaled = [panel[s] / slack[s : s + 1, rows_of(col)] for s in range(scen_local)]
    whole = jnp.concatenate(whole, axis=1)
    scaled = jnp.concatenate(scaled, axis=1)
    row = lax.broadcasted_iota(jnp.int32, (BLK, BLK), 0)
    lane = lax.broadcasted_iota(jnp.int32, (BLK, BLK), 1)
    spots = jnp.concatenate([diagonal[:, :pivot_width]] * (BLK // pivot_width), axis=1)
    index = 0
    for i in range(steps):
        wide = dot(scaled[i * BLK : (i + 1) * BLK], whole[i * BLK :], ((1,), (1,)))
        mine = (row == lane) & ((lane + i * BLK) // pivot_width == col) & (scen == 0)
        for j in range(i, steps):
            value = wide[:, (j - i) * BLK : (j - i + 1) * BLK]
            if i == j:
                value = value + jnp.where(mine, jnp.broadcast_to(spots, (BLK, BLK)), 0.0)
            gram[index * BLK : (index + 1) * BLK, :] = value
            index += 1
    if index * BLK < gram.shape[0]:
        gram[index * BLK :, :] = jnp.zeros((gram.shape[0] - index * BLK, BLK), jnp.float32)

    def half_of(side):
        return pl.ds(pl.multiple_of(side * half, 8), half)

    swap = pltpu.make_async_remote_copy(
        src_ref=gram.at[half_of(1 - core)],
        dst_ref=pair,
        send_sem=pair_sems.at[0],
        recv_sem=pair_sems.at[1],
        device_id={"col": sibling},
        device_id_type=MESH,
    )
    swap.start()
    swap.wait_recv()
    pair[...] += gram[half_of(core), :]

    def piece_of(index):
        return pl.ds(pl.multiple_of(index * piece, 8), piece)

    def spread(e):
        return pltpu.make_async_remote_copy(
            src_ref=pair.at[piece_of(lax.rem(place + e, places))],
            dst_ref=pieces.at[e - 1],
            send_sem=sum_send.at[e - 1],
            recv_sem=sum_recv.at[e - 1],
            device_id=away(e),
            device_id_type=MESH,
        )

    for e in range(1, places):
        spread(e).start()
    for e in range(1, chips):
        rhs_from(e).wait_recv()
        rhs_core(e, core).start()
    value = pair[piece_of(place), :]
    for e in range(1, places):
        spread(e).wait_recv()
        value += pieces[e - 1]

    def slot_of(index):
        return pl.ds(pl.multiple_of(core * half + index * piece, 8), piece)

    packed[slot_of(place), :] = value

    def collect(e, origin):
        return pltpu.make_async_remote_copy(
            src_ref=packed.at[slot_of(origin)],
            dst_ref=packed.at[slot_of(origin)],
            send_sem=all_send.at[e - 1],
            recv_sem=all_recv.at[e - 1],
            device_id=away(e),
            device_id_type=MESH,
        )

    for e in range(1, places):
        collect(e, place).start()
    for e in range(1, places):
        collect(e, lax.rem(place + places - e, places)).wait_recv()

    own_slack = [slack[s : s + 1, rows_of(col)] for s in range(scen_local)]

    def hop(q, origin, target, send, recv, lane=core):
        if q == 0:
            block = early.at[origin * 2 + lane]
        else:
            low_row, high_row = bounds[q - 1]
            block = held.at[origin * 2 + lane, 1:, low_row:high_row, :]
        return pltpu.make_async_remote_copy(
            src_ref=block,
            dst_ref=block,
            send_sem=send,
            recv_sem=recv.at[q, origin],
            device_id={"col": target},
            device_id_type=MESH,
        )

    def to_right(q, origin, d=1):
        return hop(q, origin, col + 2 * d, send_right.at[q, origin, d - 1], recv_right)

    def to_left(q, origin, d=1):
        return hop(q, origin, col - 2 * d, send_left.at[q, origin, d - 1], recv_left)

    def to_sibling(q, origin):
        return hop(q, origin, sibling, send_core.at[q, origin], recv_core)

    def from_sibling(q, origin):
        return hop(q, origin, sibling, send_core.at[q, origin], recv_core, 1 - core)

    def send_own(q):
        for d in (1, 2):
            @pl.when(chip + d < chips)
            def _():
                to_right(q, chip, d).start()

            @pl.when(chip >= d)
            def _():
                to_left(q, chip, d).start()

        to_sibling(q, chip).start()

    def arrive(q, distance):
        @pl.when(chip >= distance)
        def _():
            origin = chip - distance
            to_right(q, origin).wait_recv()
            if distance >= 2:
                @pl.when(chip + 1 < chips)
                def _():
                    to_right(q, origin).start()

            to_sibling(q, origin).start()

        @pl.when(chip + distance < chips)
        def _():
            origin = chip + distance
            to_left(q, origin).wait_recv()
            if distance >= 2:
                @pl.when(chip > 0)
                def _():
                    to_left(q, origin).start()

            to_sibling(q, origin).start()

    def finish(side):
        return pltpu.make_async_remote_copy(
            src_ref=packed.at[half_of(side)],
            dst_ref=packed.at[half_of(side)],
            send_sem=core_sems.at[0],
            recv_sem=core_sems.at[1],
            device_id={"col": sibling},
            device_id_type=MESH,
        )

    finish(core).start()
    early[col] = panel[0, :, :BLK]
    send_own(0)
    for e in range(chips):
        rhs_core(e, 1 - core).wait_recv()
    finish(1 - core).wait_recv()
    for t in range(col_count):
        if t != here:
            hand_out(t).wait_send()
    for e in range(1, chips):
        rhs_away(e).wait_send()
    for e in range(chips):
        rhs_core(e, core).wait_send()
    swap.wait_send()
    for e in range(1, places):
        spread(e).wait_send()
        collect(e, place).wait_send()
    finish(core).wait_send()

    matrix[...] = jnp.zeros_like(matrix)
    for index, (i, j) in enumerate(blocks_of(steps)):
        matrix[i * BLK : (i + 1) * BLK, j * BLK : (j + 1) * BLK] = packed[index * BLK : (index + 1) * BLK, :]
    hops = chips - 1

    def between(step):
        if 1 <= step and step < hops:
            arrive(0, step)

    factor_and_solve(matrix, rhs_panel, forward, solved, upper, inverses, between)

    def own_rows(q):
        low_row, high_row = bounds[q - 1]
        for s in range(scen_local):
            moved = dot(solved[:, low_row:high_row], panel[s], ((0,), (0,)))
            scaled = moved / own_slack[s]
            for r in range(pieces_per_row):
                held[col, s * pieces_per_row + r, low_row:high_row, :] = scaled[:, r * BLK : (r + 1) * BLK]
            directions[s, :, low_row:high_row] = moved.T

    def early_rows(t):
        owner = lax.rem(col + t, col_count)
        moved = dot(solved[...], early[owner], ((0,), (0,)))
        held[owner, 0] = moved / slack[0:1, pl.ds(pl.multiple_of(owner * row_share, row_share), BLK)]

    width = own_share

    def multiply(q, origin, first, last):
        low_row, high_row = bounds[q - 1]
        count = high_row - low_row
        for k in range(2):
            for part in range(parts):
                top, rest = halves(held[origin * 2 + k, part, low_row:high_row, :])
                s, r = part // pieces_per_row, part % pieces_per_row
                lanes = slice((s * 2 + k) * row_share + r * BLK, (s * 2 + k) * row_share + (r + 1) * BLK)
                split[:count, lanes] = top
                split[count : 2 * count, lanes] = rest
        rows = pl.ds(pl.multiple_of(origin * chip_rows, chip_rows), chip_rows)

        def body(t, carry):
            peer = lax.rem(scen + 1 + t, scen_count)
            lanes = pl.ds(pl.multiple_of(peer * width, width), width)
            both = jnp.dot(split[: 2 * count], high[rows, lanes], preferred_element_type=jnp.float32)
            value = both[:count] + both[count:]
            value += jnp.dot(split[:count], low[rows, lanes], preferred_element_type=jnp.float32)
            if first:
                total[low_row:high_row, lanes] = value
            else:
                total[low_row:high_row, lanes] += value

                @pl.when(last & (t + 1 < scen_count))
                def _():
                    share(q, t + 1).start()

            return carry

        lax.fori_loop(0, scen_count, body, 0)

    def add_in(q, distance):
        if distance == 0:
            from_sibling(q, chip).wait_recv()
            multiply(q, chip, True, False)
            return

        furthest = jnp.maximum(chip, chips - 1 - chip)
        rightmost = chips - 1 - chip == furthest

        @pl.when(chip >= distance)
        def _():
            from_sibling(q, chip - distance).wait_recv()
            multiply(q, chip - distance, False, (distance == furthest) & jnp.logical_not(rightmost))

        @pl.when(chip + distance < chips)
        def _():
            from_sibling(q, chip + distance).wait_recv()
            multiply(q, chip + distance, False, (distance == furthest) & rightmost)

    def share(q, d):
        low_row, high_row = bounds[q - 1]
        peer = lax.rem(scen + d, scen_count)
        return pltpu.make_async_remote_copy(
            src_ref=total.at[low_row:high_row, pl.ds(pl.multiple_of(peer * own_share, own_share), own_share)],
            dst_ref=landed.at[d - 1, low_row:high_row],
            send_sem=scen_send.at[q - 1, d - 1],
            recv_sem=scen_recv.at[q - 1, d - 1],
            device_id={"scen": peer},
            device_id_type=MESH,
        )

    def finish_chunk(q):
        low_row, high_row = bounds[q - 1]
        value = total[low_row:high_row, pl.ds(pl.multiple_of(scen * own_share, own_share), own_share)]
        for d in range(1, scen_count):
            share(q, d).wait_recv()
            value += landed[d - 1, low_row:high_row]
        reduced[:, low_row:high_row] = rhs_rows[:, low_row:high_row] - value.T

    chunks = len(bounds)
    own_rows(1)
    send_own(1)
    for distance in range(min(3, hops), chips):
        arrive(0, distance)
    for q in range(2, chunks + 1):
        own_rows(q)
    for distance in range(chips):
        if distance == 0:
            from_sibling(0, chip).wait_recv()
        else:
            @pl.when(chip >= distance)
            def _():
                from_sibling(0, chip - distance).wait_recv()

            @pl.when(chip + distance < chips)
            def _():
                from_sibling(0, chip + distance).wait_recv()

    def every(t, carry):
        early_rows(t)
        return carry

    lax.fori_loop(1, col_count, every, 0)
    rhs_copy.wait()
    for q in range(1, chunks + 1):
        for distance in range(chips):
            if distance + 1 < chips:
                arrive(q, distance + 1)
            if distance == 0 and q < chunks:
                send_own(q + 1)
            add_in(q, distance)
        if q == 1:
            for s in range(scen_local):
                directions[s] = (scen_rhs[s] - directions[s]) / own_slack[s].T
        else:
            finish_chunk(q - 1)
    finish_chunk(chunks)

    @pl.when(scen == 0)
    def _():
        reduced[:pivot_width, :] = forward[pivots_of(col), :]

    for q in range(chunks + 1):
        for d in (1, 2):
            @pl.when(chip + d < chips)
            def _():
                to_right(q, chip, d).wait_send()

            @pl.when(chip >= d)
            def _():
                to_left(q, chip, d).wait_send()

        for distance in range(2, chips):
            @pl.when((chip >= distance) & (chip + 1 < chips))
            def _():
                to_right(q, chip - distance).wait_send()

            @pl.when((chip + distance < chips) & (chip > 0))
            def _():
                to_left(q, chip + distance).wait_send()

        for origin in range(chips):
            to_sibling(q, origin).wait_send()
        if q > 0:
            for d in range(1, scen_count):
                share(q, d).wait_send()


def chunk_bounds(rhs_count):
    bounds, done = [], 0
    for share in CHUNKS:
        bounds.append((done, done + rhs_count // share))
        done += rhs_count // share
    return bounds


def eliminate_panel(slack, pattern, diagonal, scen_rhs, border, rhs):
    scen_count = lax.axis_size("scen")
    col_count = lax.axis_size("col")
    chips = col_count // 2
    places = scen_count * chips
    scen_local, row_total, own_width = border.shape
    row_blocks = pattern.shape[1]
    row_share = row_total // col_count
    own_share = own_width // scen_count
    pivot_width = PW // col_count
    rhs_count = rhs.shape[1]
    chunks = len(CHUNKS)
    largest = rhs_count // min(CHUNKS)
    lanes_read = -(-pivot_width // BLK) * BLK
    count = len(blocks_of(PW // BLK)) * BLK
    piece = -(-count // (2 * places * 8)) * 8
    half = piece * places
    vmem = pl.BlockSpec(memory_space=pltpu.VMEM)
    hbm = pl.BlockSpec(memory_space=pl.ANY)
    dma = pltpu.SemaphoreType.DMA

    def floats(*shape):
        return pltpu.VMEM(shape, jnp.float32)

    return pl.pallas_call(
        functools.partial(whole_kernel, (scen_count, col_count)),
        in_specs=[vmem] * 4 + [hbm] * 2,
        out_specs=[vmem] * 2,
        out_shape=(
            jax.ShapeDtypeStruct((own_share, rhs_count), jnp.float32),
            jax.ShapeDtypeStruct(scen_rhs.shape, jnp.float32),
        ),
        scratch_shapes=[
            floats(scen_local, PW, row_share),
            floats(2 * half, BLK),
            floats(PW, rhs_count),
            floats(col_count, scen_local, row_share, lanes_read),
            floats(col_count, scen_local, pivot_width, row_share),
            floats(2 * half, BLK),
            floats(half, BLK),
            floats(places - 1, piece, BLK),
            floats(PW, PW),
            floats(PW, PW),
            floats(PW, BLK),
            floats(PW, rhs_count),
            floats(PW, rhs_count),
            floats(scen_local, row_blocks, 1, own_width),
            floats(col_count, PW, BLK),
            floats(STAGES, row_total // row_blocks, own_width),
            pltpu.VMEM((scen_local * row_total, own_width), jnp.bfloat16),
            pltpu.VMEM((scen_local * row_total, own_width), jnp.bfloat16),
            floats(col_count, scen_local * row_share // BLK, rhs_count, BLK),
            pltpu.VMEM((2 * largest, 2 * scen_local * row_share), jnp.bfloat16),
            floats(rhs_count, own_width),
            floats(scen_count - 1, rhs_count, own_share),
            floats(own_share, rhs_count),
            dma((col_count,)),
            dma,
            dma((col_count,)),
            dma((col_count,)),
            dma((chips - 1,)),
            dma((chips - 1,)),
            dma((chips,)),
            dma((chips,)),
            dma((2,)),
            dma((places - 1,)),
            dma((places - 1,)),
            dma((places - 1,)),
            dma((places - 1,)),
            dma((2,)),
            dma((STAGES,)),
            dma,
            dma((chunks + 1, chips, 2)),
            dma((chunks + 1, chips, 2)),
            dma((chunks + 1, chips)),
            dma((chunks + 1, chips)),
            dma((chunks + 1, chips)),
            dma((chunks + 1, chips)),
            dma((chunks, scen_count - 1)),
            dma((chunks, scen_count - 1)),
        ],
        compiler_params=pltpu.CompilerParams(
            collective_id=0, has_side_effects=True, vmem_limit_bytes=63 << 20
        ),
        cost_estimate=pl.CostEstimate(
            flops=6 * scen_local * row_total * own_width * rhs_count,
            bytes_accessed=4 * scen_local * row_total * own_width,
            transcendentals=0,
        ),
    )(slack, pattern, diagonal, scen_rhs, border, rhs)


def hand_over_kernel(reduced, directions, reduced_out, directions_out, sems):
    copies = [
        pltpu.make_async_copy(reduced, reduced_out, sems.at[0]),
        pltpu.make_async_copy(directions, directions_out, sems.at[1]),
    ]
    for copy in copies:
        copy.start()
    for copy in copies:
        copy.wait()


def hand_over(*arrays):
    hbm = pl.BlockSpec(memory_space=pl.ANY)
    return pl.pallas_call(
        hand_over_kernel,
        in_specs=[hbm] * 2,
        out_specs=[hbm] * 2,
        out_shape=tuple(jax.ShapeDtypeStruct(x.shape, x.dtype) for x in arrays),
        scratch_shapes=[pltpu.SemaphoreType.DMA((2,))],
    )(*arrays)


def per_device(border, pattern, slack, first_diag, rhs, scen_rhs):
    reduced, directions = hand_over(
        *eliminate_panel(slack, pattern, first_diag[None, :], scen_rhs, border, rhs)
    )
    return reduced[None], directions


def solution(mesh):
    return jax.shard_map(
        per_device,
        mesh=mesh,
        in_specs=(
            P("scen", None, "col"),
            P("scen", None, "col"),
            P("scen", None),
            P("col"),
            P("col", None),
            P("scen", "col", None),
        ),
        out_specs=(P("col", "scen", None), P("scen", "col", None)),
        check_vma=False,
    )
```

```python
import functools

import jax
import jax.numpy as jnp
from jax import lax
from jax.experimental import pallas as pl
from jax.experimental.pallas import tpu as pltpu
from jax.sharding import PartitionSpec as P

PW = 512
BLK = 128
HIGHEST = lax.Precision.HIGHEST
MESH = pl.DeviceIdType.MESH
CHUNKS = (2, 2)
STAGES = 2


def dot(a, b, contract=((1,), (0,))):
    return lax.dot_general(
        a, b, (contract, ((), ())), precision=HIGHEST, preferred_element_type=jnp.float32
    )


def halves(x):
    high = x.astype(jnp.bfloat16)
    return high, (x - high.astype(jnp.float32)).astype(jnp.bfloat16)


def blocks_of(steps):
    return [(i, j) for i in range(steps) for j in range(i, steps)]


def invert_factor(block):
    groups = BLK // 8
    shape = (8, BLK)
    sub = lax.broadcasted_iota(jnp.int32, shape, 0)
    lane = lax.broadcasted_iota(jnp.int32, shape, 1)
    rows = [block[8 * i : 8 * i + 8, :] for i in range(groups)]
    inverse = [jnp.where(lane == sub + 8 * i, 1.0, 0.0).astype(jnp.float32) for i in range(groups)]
    for g in range(groups):
        columns = [
            {i: jnp.broadcast_to(rows[i][:, 8 * g + m : 8 * g + m + 1], shape) for i in range(g, groups)}
            for m in range(8)
        ]
        pivots = jnp.ones(shape, jnp.float32)
        for m in range(8):
            head = columns[m][g]
            pivot = jnp.broadcast_to(head[m : m + 1, :], shape)
            scale = 1.0 / pivot
            pivots = jnp.where(sub == m, pivot, pivots)
            row = jnp.broadcast_to(rows[g][m : m + 1, :], shape) * scale
            inverse_row = jnp.broadcast_to(inverse[g][m : m + 1, :], shape) * scale
            factors = [
                jnp.broadcast_to(head[later : later + 1, :], shape) * scale for later in range(m + 1, 8)
            ]
            for i in range(g, groups):
                column = columns[m][i]
                if i == g:
                    column = jnp.where(sub > m, column, 0.0)
                rows[i] = rows[i] - column * row
                inverse[i] = inverse[i] - column * inverse_row
                for later in range(m + 1, 8):
                    columns[later][i] = columns[later][i] - column * factors[later - m - 1]
        inverse[g] = inverse[g] * lax.rsqrt(pivots)
    return jnp.concatenate(inverse, axis=0)


def factor_and_solve(matrix, right, forward, solved, upper, inverses, between):
    steps = matrix.shape[0] // BLK

    def block(i):
        return slice(i * BLK, (i + 1) * BLK)

    def eliminate(j, carry):
        here = pl.ds(pl.multiple_of(j * BLK, BLK), BLK)
        inverse = invert_factor(matrix[here, here])
        inverses[here, :] = inverse
        forward[here, :] = dot(inverse, right[here, :])
        for now in range(steps - 1):
            @pl.when(j == now)
            def _():
                wide = dot(inverse, matrix[block(now), (now + 1) * BLK :])
                upper[block(now), (now + 1) * BLK :] = wide
                for i in range(now + 1, steps):
                    rows = wide[:, (i - now - 1) * BLK : (i - now) * BLK]
                    matrix[block(i), i * BLK :] -= dot(rows, wide[:, (i - now - 1) * BLK :], ((0,), (0,)))
                right[(now + 1) * BLK :, :] -= dot(wide, forward[block(now), :], ((0,), (0,)))
                between(now)
        return carry

    lax.fori_loop(0, steps, eliminate, 0)
    for j in reversed(range(steps)):
        rest = forward[block(j), :]
        if j + 1 < steps:
            rest = rest - dot(upper[block(j), (j + 1) * BLK :], solved[(j + 1) * BLK :, :])
        solved[block(j), :] = dot(inverses[block(j), :], rest, ((0,), (0,)))


def whole_kernel(
    mesh_sizes, slack, pattern, diagonal, scen_rhs, border, rhs, reduced, directions,
    panel, packed, rhs_panel, raw, sent, gram, pair, pieces, matrix, upper, inverses, forward, solved,
    mask, early, stage, high, low, held, split, total, landed, rhs_rows,
    raw_sem, rhs_sem, out_send, out_recv, rhs_send, rhs_recv, rhs_core_send, rhs_core_recv,
    pair_sems, sum_send, sum_recv, all_send, all_recv, core_sems,
    stage_sem, own_rhs_sem, send_right, send_left, send_core, recv_right, recv_left, recv_core,
    scen_send, scen_recv,
):
    scen_count, col_count = mesh_sizes
    chips = col_count // 2
    places = scen_count * chips
    scen = lax.axis_index("scen")
    col = lax.axis_index("col")
    chip, core = col // 2, col % 2
    sibling = chip * 2 + (1 - core)
    place = scen * chips + chip
    scen_local, pw, row_share = panel.shape
    row_blocks, width_blocks = pattern.shape[1:]
    row_block = border.shape[1] // row_blocks
    col_block = border.shape[2] // width_blocks
    pivot_width = pw // col_count
    lanes_read = raw.shape[3]
    piece = pieces.shape[1]
    half = piece * places

    def target(t):
        return lax.rem(col + col_count // 2 + t, col_count)

    def rows_of(owner):
        return pl.ds(pl.multiple_of(owner * row_share, row_share), row_share)

    def pivots_of(owner):
        return pl.ds(pl.multiple_of(owner * pivot_width, pivot_width), pivot_width)

    def read(t):
        return pltpu.make_async_copy(
            border.at[:, rows_of(target(t)), pl.ds(0, lanes_read)], raw.at[t], raw_sem.at[t]
        )

    for t in range(col_count):
        read(t).start()
    own_rhs = pltpu.make_async_copy(rhs.at[pl.ds(0, pivot_width)], rhs_panel.at[pivots_of(col)], rhs_sem)
    own_rhs.start()

    own_width = border.shape[2]
    own_share = own_width // scen_count
    bounds = chunk_bounds(rhs.shape[1])
    pieces_per_row = row_share // BLK
    parts = scen_local * pieces_per_row
    blocks = border.shape[1] // row_block
    units = scen_local * blocks
    chip_rows = 2 * scen_local * row_share

    def border_copy(unit):
        scenario, block = unit // blocks, unit % blocks
        slot = unit % STAGES
        return pltpu.make_async_copy(
            border.at[scenario, pl.ds(pl.multiple_of(block * row_block, row_block), row_block)],
            stage.at[slot],
            stage_sem.at[slot],
        )

    for unit in range(STAGES):
        border_copy(unit).start()
    rhs_copy = pltpu.make_async_copy(
        rhs.at[pl.ds(pl.multiple_of(scen * own_share, own_share), own_share)], rhs_rows, own_rhs_sem
    )
    rhs_copy.start()

    def convert(begin, end):
        def body(unit, carry):
            scenario, block = unit // blocks, unit % blocks
            slot = unit % STAGES
            owner = block * row_block // row_share
            place = (owner // 2 * scen_local + scenario) * 2 + owner % 2
            base = place * row_share + block * row_block % row_share
            border_copy(unit).wait()
            weight = mask[scenario, block]

            def some(t, inner):
                value = stage[slot, pl.ds(pl.multiple_of(t * 16, 16), 16), :] * weight
                top = value.astype(jnp.bfloat16)
                here = pl.ds(pl.multiple_of(base + t * 16, 16), 16)
                high[here, :] = top
                low[here, :] = (value - top.astype(jnp.float32)).astype(jnp.bfloat16)
                return inner

            lax.fori_loop(0, row_block // 16, some, 0)

            @pl.when(unit + STAGES < units)
            def _():
                border_copy(unit + STAGES).start()

            return carry

        lax.fori_loop(begin, end, body, 0)

    barrier = pltpu.get_barrier_semaphore()

    def greet(device):
        pl.semaphore_signal(barrier, inc=1, device_id=device, device_id_type=MESH)

    def away(e):
        other = lax.rem(place + e, places)
        return {"scen": other // chips, "col": lax.rem(other, chips) * 2 + core}

    def across(e):
        return {"col": lax.rem(chip + e, chips) * 2 + (1 - core)}

    for e in range(1, places):
        greet(away(e))
    for e in range(chips):
        greet(across(e))

    for s in range(scen_local):
        ones = pattern[s].astype(jnp.float32)
        wide = [jnp.broadcast_to(ones[:, c : c + 1], (row_blocks, col_block)) for c in range(width_blocks)]
        wide = jnp.concatenate(wide, axis=1)
        for r in range(row_blocks):
            mask[s, r] = wide[r : r + 1]

    def hand_out(t):
        return pltpu.make_async_remote_copy(
            src_ref=sent.at[t],
            dst_ref=panel.at[:, pivots_of(col), :],
            send_sem=out_send.at[t],
            recv_sem=out_recv.at[t],
            device_id={"col": target(t)},
            device_id_type=MESH,
        )

    def hand_in(t):
        source = lax.rem(col + 2 * col_count - col_count // 2 - t, col_count)
        return pltpu.make_async_remote_copy(
            src_ref=sent.at[t],
            dst_ref=panel.at[:, pivots_of(source), :],
            send_sem=out_send.at[t],
            recv_sem=out_recv.at[t],
            device_id={"col": source},
            device_id_type=MESH,
        )

    here = col_count - col_count // 2
    for t in range(col_count):
        read(t).wait()
        for s in range(scen_local):
            for r in range(row_share // row_block):
                weight = mask[s, target(t) * (row_share // row_block) + r, :, :lanes_read]
                value = raw[t, s, r * row_block : (r + 1) * row_block, :] * weight
                value = value.T[:pivot_width]
                if t == here:
                    panel[s, pivots_of(col), r * row_block : (r + 1) * row_block] = value
                else:
                    sent[t, s, :, r * row_block : (r + 1) * row_block] = value
        if t == 0:
            pl.semaphore_wait(barrier, places - 1 + chips)
        if t != here:
            hand_out(t).start()

    def rhs_away(e, origin_shift=0):
        return pltpu.make_async_remote_copy(
            src_ref=rhs_panel.at[pivots_of(col)],
            dst_ref=rhs_panel.at[pivots_of(col)],
            send_sem=rhs_send.at[e - 1],
            recv_sem=rhs_recv.at[e - 1],
            device_id={"col": lax.rem(chip + e, chips) * 2 + core},
            device_id_type=MESH,
        )

    def rhs_from(e):
        source = lax.rem(chip + chips - e, chips) * 2 + core
        return pltpu.make_async_remote_copy(
            src_ref=rhs_panel.at[pivots_of(source)],
            dst_ref=rhs_panel.at[pivots_of(source)],
            send_sem=rhs_send.at[e - 1],
            recv_sem=rhs_recv.at[e - 1],
            device_id={"col": source},
            device_id_type=MESH,
        )

    def rhs_core(e, side):
        owner = lax.rem(chip + chips - e, chips) * 2 + side
        return pltpu.make_async_remote_copy(
            src_ref=rhs_panel.at[pivots_of(owner)],
            dst_ref=rhs_panel.at[pivots_of(owner)],
            send_sem=rhs_core_send.at[e],
            recv_sem=rhs_core_recv.at[e],
            device_id={"col": sibling},
            device_id_type=MESH,
        )

    convert(0, units)
    for t in range(col_count):
        if t != here:
            hand_in(t).wait_recv()

    own_rhs.wait()
    for e in range(1, chips):
        rhs_away(e).start()
    rhs_core(0, core).start()

    steps = pw // BLK
    whole = [panel[s] for s in range(scen_local)]
    scaled = [panel[s] / slack[s : s + 1, rows_of(col)] for s in range(scen_local)]
    whole = jnp.concatenate(whole, axis=1)
    scaled = jnp.concatenate(scaled, axis=1)
    row = lax.broadcasted_iota(jnp.int32, (BLK, BLK), 0)
    lane = lax.broadcasted_iota(jnp.int32, (BLK, BLK), 1)
    spots = jnp.concatenate([diagonal[:, :pivot_width]] * (BLK // pivot_width), axis=1)
    index = 0
    for i in range(steps):
        wide = dot(scaled[i * BLK : (i + 1) * BLK], whole[i * BLK :], ((1,), (1,)))
        mine = (row == lane) & ((lane + i * BLK) // pivot_width == col) & (scen == 0)
        for j in range(i, steps):
            value = wide[:, (j - i) * BLK : (j - i + 1) * BLK]
            if i == j:
                value = value + jnp.where(mine, jnp.broadcast_to(spots, (BLK, BLK)), 0.0)
            gram[index * BLK : (index + 1) * BLK, :] = value
            index += 1
    if index * BLK < gram.shape[0]:
        gram[index * BLK :, :] = jnp.zeros((gram.shape[0] - index * BLK, BLK), jnp.float32)

    def half_of(side):
        return pl.ds(pl.multiple_of(side * half, 8), half)

    swap = pltpu.make_async_remote_copy(
        src_ref=gram.at[half_of(1 - core)],
        dst_ref=pair,
        send_sem=pair_sems.at[0],
        recv_sem=pair_sems.at[1],
        device_id={"col": sibling},
        device_id_type=MESH,
    )
    swap.start()
    swap.wait_recv()
    pair[...] += gram[half_of(core), :]

    def piece_of(index):
        return pl.ds(pl.multiple_of(index * piece, 8), piece)

    def spread(e):
        return pltpu.make_async_remote_copy(
            src_ref=pair.at[piece_of(lax.rem(place + e, places))],
            dst_ref=pieces.at[e - 1],
            send_sem=sum_send.at[e - 1],
            recv_sem=sum_recv.at[e - 1],
            device_id=away(e),
            device_id_type=MESH,
        )

    for e in range(1, places):
        spread(e).start()
    for e in range(1, chips):
        rhs_from(e).wait_recv()
        rhs_core(e, core).start()
    value = pair[piece_of(place), :]
    for e in range(1, places):
        spread(e).wait_recv()
        value += pieces[e - 1]

    def slot_of(index):
        return pl.ds(pl.multiple_of(core * half + index * piece, 8), piece)

    packed[slot_of(place), :] = value

    def collect(e, origin):
        return pltpu.make_async_remote_copy(
            src_ref=packed.at[slot_of(origin)],
            dst_ref=packed.at[slot_of(origin)],
            send_sem=all_send.at[e - 1],
            recv_sem=all_recv.at[e - 1],
            device_id=away(e),
            device_id_type=MESH,
        )

    for e in range(1, places):
        collect(e, place).start()
    for e in range(1, places):
        collect(e, lax.rem(place + places - e, places)).wait_recv()

    own_slack = [slack[s : s + 1, rows_of(col)] for s in range(scen_local)]

    def hop(q, origin, target, send, recv, lane=core):
        if q == 0:
            block = early.at[origin * 2 + lane]
        else:
            low_row, high_row = bounds[q - 1]
            block = held.at[origin * 2 + lane, 1:, low_row:high_row, :]
        return pltpu.make_async_remote_copy(
            src_ref=block,
            dst_ref=block,
            send_sem=send,
            recv_sem=recv.at[q, origin],
            device_id={"col": target},
            device_id_type=MESH,
        )

    def to_right(q, origin, d=1):
        return hop(q, origin, col + 2 * d, send_right.at[q, origin, d - 1], recv_right)

    def to_left(q, origin, d=1):
        return hop(q, origin, col - 2 * d, send_left.at[q, origin, d - 1], recv_left)

    def to_sibling(q, origin):
        return hop(q, origin, sibling, send_core.at[q, origin], recv_core)

    def from_sibling(q, origin):
        return hop(q, origin, sibling, send_core.at[q, origin], recv_core, 1 - core)

    def send_own(q):
        for d in (1, 2):
            @pl.when(chip + d < chips)
            def _():
                to_right(q, chip, d).start()

            @pl.when(chip >= d)
            def _():
                to_left(q, chip, d).start()

        to_sibling(q, chip).start()

    def arrive(q, distance):
        @pl.when(chip >= distance)
        def _():
            origin = chip - distance
            to_right(q, origin).wait_recv()
            if distance >= 2:
                @pl.when(chip + 1 < chips)
                def _():
                    to_right(q, origin).start()

            to_sibling(q, origin).start()

        @pl.when(chip + distance < chips)
        def _():
            origin = chip + distance
            to_left(q, origin).wait_recv()
            if distance >= 2:
                @pl.when(chip > 0)
                def _():
                    to_left(q, origin).start()

            to_sibling(q, origin).start()

    def finish(side):
        return pltpu.make_async_remote_copy(
            src_ref=packed.at[half_of(side)],
            dst_ref=packed.at[half_of(side)],
            send_sem=core_sems.at[0],
            recv_sem=core_sems.at[1],
            device_id={"col": sibling},
            device_id_type=MESH,
        )

    finish(core).start()
    early[col] = panel[0, :, :BLK]
    send_own(0)
    for e in range(chips):
        rhs_core(e, 1 - core).wait_recv()
    finish(1 - core).wait_recv()
    for t in range(col_count):
        if t != here:
            hand_out(t).wait_send()
    for e in range(1, chips):
        rhs_away(e).wait_send()
    for e in range(chips):
        rhs_core(e, core).wait_send()
    swap.wait_send()
    for e in range(1, places):
        spread(e).wait_send()
        collect(e, place).wait_send()
    finish(core).wait_send()

    matrix[...] = jnp.zeros_like(matrix)
    for index, (i, j) in enumerate(blocks_of(steps)):
        matrix[i * BLK : (i + 1) * BLK, j * BLK : (j + 1) * BLK] = packed[index * BLK : (index + 1) * BLK, :]
    hops = chips - 1

    def between(step):
        if 1 <= step and step < hops:
            arrive(0, step)

    factor_and_solve(matrix, rhs_panel, forward, solved, upper, inverses, between)

    def own_rows(q):
        low_row, high_row = bounds[q - 1]
        for s in range(scen_local):
            moved = dot(solved[:, low_row:high_row], panel[s], ((0,), (0,)))
            scaled = moved / own_slack[s]
            for r in range(pieces_per_row):
                held[col, s * pieces_per_row + r, low_row:high_row, :] = scaled[:, r * BLK : (r + 1) * BLK]
            directions[s, :, low_row:high_row] = moved.T

    def early_rows(t):
        owner = lax.rem(col + t, col_count)
        moved = dot(solved[...], early[owner], ((0,), (0,)))
        held[owner, 0] = moved / slack[0:1, pl.ds(pl.multiple_of(owner * row_share, row_share), BLK)]

    width = own_share

    def multiply(q, origin, first, last):
        low_row, high_row = bounds[q - 1]
        count = high_row - low_row
        for k in range(2):
            for part in range(parts):
                top, rest = halves(held[origin * 2 + k, part, low_row:high_row, :])
                s, r = part // pieces_per_row, part % pieces_per_row
                lanes = slice((s * 2 + k) * row_share + r * BLK, (s * 2 + k) * row_share + (r + 1) * BLK)
                split[:count, lanes] = top
                split[count : 2 * count, lanes] = rest
        rows = pl.ds(pl.multiple_of(origin * chip_rows, chip_rows), chip_rows)

        def body(t, carry):
            peer = lax.rem(scen + 1 + t, scen_count)
            lanes = pl.ds(pl.multiple_of(peer * width, width), width)
            both = jnp.dot(split[: 2 * count], high[rows, lanes], preferred_element_type=jnp.float32)
            value = both[:count] + both[count:]
            value += jnp.dot(split[:count], low[rows, lanes], preferred_element_type=jnp.float32)
            if first:
                total[low_row:high_row, lanes] = value
            else:
                total[low_row:high_row, lanes] += value

                @pl.when(last & (t + 1 < scen_count))
                def _():
                    share(q, t + 1).start()

            return carry

        lax.fori_loop(0, scen_count, body, 0)

    def add_in(q, distance):
        if distance == 0:
            from_sibling(q, chip).wait_recv()
            multiply(q, chip, True, False)
            return

        furthest = jnp.maximum(chip, chips - 1 - chip)
        rightmost = chips - 1 - chip == furthest

        @pl.when(chip >= distance)
        def _():
            from_sibling(q, chip - distance).wait_recv()
            multiply(q, chip - distance, False, (distance == furthest) & jnp.logical_not(rightmost))

        @pl.when(chip + distance < chips)
        def _():
            from_sibling(q, chip + distance).wait_recv()
            multiply(q, chip + distance, False, (distance == furthest) & rightmost)

    def share(q, d):
        low_row, high_row = bounds[q - 1]
        peer = lax.rem(scen + d, scen_count)
        return pltpu.make_async_remote_copy(
            src_ref=total.at[low_row:high_row, pl.ds(pl.multiple_of(peer * own_share, own_share), own_share)],
            dst_ref=landed.at[d - 1, low_row:high_row],
            send_sem=scen_send.at[q - 1, d - 1],
            recv_sem=scen_recv.at[q - 1, d - 1],
            device_id={"scen": peer},
            device_id_type=MESH,
        )

    def finish_chunk(q):
        low_row, high_row = bounds[q - 1]
        value = total[low_row:high_row, pl.ds(pl.multiple_of(scen * own_share, own_share), own_share)]
        for d in range(1, scen_count):
            share(q, d).wait_recv()
            value += landed[d - 1, low_row:high_row]
        reduced[:, low_row:high_row] = rhs_rows[:, low_row:high_row] - value.T

    chunks = len(bounds)
    own_rows(1)
    send_own(1)
    for distance in range(min(3, hops), chips):
        arrive(0, distance)
    for q in range(2, chunks + 1):
        own_rows(q)
    for distance in range(chips):
        if distance == 0:
            from_sibling(0, chip).wait_recv()
        else:
            @pl.when(chip >= distance)
            def _():
                from_sibling(0, chip - distance).wait_recv()

            @pl.when(chip + distance < chips)
            def _():
                from_sibling(0, chip + distance).wait_recv()

    def every(t, carry):
        early_rows(t)
        return carry

    lax.fori_loop(1, col_count, every, 0)
    rhs_copy.wait()
    for q in range(1, chunks + 1):
        for distance in range(chips):
            if distance + 1 < chips:
                arrive(q, distance + 1)
            if distance == 0 and q < chunks:
                send_own(q + 1)
            add_in(q, distance)
        if q == 1:
            for s in range(scen_local):
                directions[s] = (scen_rhs[s] - directions[s]) / own_slack[s].T
        else:
            finish_chunk(q - 1)
    finish_chunk(chunks)

    @pl.when(scen == 0)
    def _():
        reduced[:pivot_width, :] = forward[pivots_of(col), :]

    for q in range(chunks + 1):
        for d in (1, 2):
            @pl.when(chip + d < chips)
            def _():
                to_right(q, chip, d).wait_send()

            @pl.when(chip >= d)
            def _():
                to_left(q, chip, d).wait_send()

        for distance in range(2, chips):
            @pl.when((chip >= distance) & (chip + 1 < chips))
            def _():
                to_right(q, chip - distance).wait_send()

            @pl.when((chip + distance < chips) & (chip > 0))
            def _():
                to_left(q, chip + distance).wait_send()

        for origin in range(chips):
            to_sibling(q, origin).wait_send()
        if q > 0:
            for d in range(1, scen_count):
                share(q, d).wait_send()


def chunk_bounds(rhs_count):
    bounds, done = [], 0
    for share in CHUNKS:
        bounds.append((done, done + rhs_count // share))
        done += rhs_count // share
    return bounds


def eliminate_panel(slack, pattern, diagonal, scen_rhs, border, rhs):
    scen_count = lax.axis_size("scen")
    col_count = lax.axis_size("col")
    chips = col_count // 2
    places = scen_count * chips
    scen_local, row_total, own_width = border.shape
    row_blocks = pattern.shape[1]
    row_share = row_total // col_count
    own_share = own_width // scen_count
    pivot_width = PW // col_count
    rhs_count = rhs.shape[1]
    chunks = len(CHUNKS)
    largest = rhs_count // min(CHUNKS)
    lanes_read = -(-pivot_width // BLK) * BLK
    count = len(blocks_of(PW // BLK)) * BLK
    piece = -(-count // (2 * places * 8)) * 8
    half = piece * places
    vmem = pl.BlockSpec(memory_space=pltpu.VMEM)
    hbm = pl.BlockSpec(memory_space=pl.ANY)
    dma = pltpu.SemaphoreType.DMA

    def floats(*shape):
        return pltpu.VMEM(shape, jnp.float32)

    return pl.pallas_call(
        functools.partial(whole_kernel, (scen_count, col_count)),
        in_specs=[vmem] * 4 + [hbm] * 2,
        out_specs=[vmem] * 2,
        out_shape=(
            jax.ShapeDtypeStruct((own_share, rhs_count), jnp.float32),
            jax.ShapeDtypeStruct(scen_rhs.shape, jnp.float32),
        ),
        scratch_shapes=[
            floats(scen_local, PW, row_share),
            floats(2 * half, BLK),
            floats(PW, rhs_count),
            floats(col_count, scen_local, row_share, lanes_read),
            floats(col_count, scen_local, pivot_width, row_share),
            floats(2 * half, BLK),
            floats(half, BLK),
            floats(places - 1, piece, BLK),
            floats(PW, PW),
            floats(PW, PW),
            floats(PW, BLK),
            floats(PW, rhs_count),
            floats(PW, rhs_count),
            floats(scen_local, row_blocks, 1, own_width),
            floats(col_count, PW, BLK),
            floats(STAGES, row_total // row_blocks, own_width),
            pltpu.VMEM((scen_local * row_total, own_width), jnp.bfloat16),
            pltpu.VMEM((scen_local * row_total, own_width), jnp.bfloat16),
            floats(col_count, scen_local * row_share // BLK, rhs_count, BLK),
            pltpu.VMEM((2 * largest, 2 * scen_local * row_share), jnp.bfloat16),
            floats(rhs_count, own_width),
            floats(scen_count - 1, rhs_count, own_share),
            floats(own_share, rhs_count),
            dma((col_count,)),
            dma,
            dma((col_count,)),
            dma((col_count,)),
            dma((chips - 1,)),
            dma((chips - 1,)),
            dma((chips,)),
            dma((chips,)),
            dma((2,)),
            dma((places - 1,)),
            dma((places - 1,)),
            dma((places - 1,)),
            dma((places - 1,)),
            dma((2,)),
            dma((STAGES,)),
            dma,
            dma((chunks + 1, chips, 2)),
            dma((chunks + 1, chips, 2)),
            dma((chunks + 1, chips)),
            dma((chunks + 1, chips)),
            dma((chunks + 1, chips)),
            dma((chunks + 1, chips)),
            dma((chunks, scen_count - 1)),
            dma((chunks, scen_count - 1)),
        ],
        compiler_params=pltpu.CompilerParams(
            collective_id=0, has_side_effects=True, vmem_limit_bytes=63 << 20
        ),
        cost_estimate=pl.CostEstimate(
            flops=6 * scen_local * row_total * own_width * rhs_count,
            bytes_accessed=4 * scen_local * row_total * own_width,
            transcendentals=0,
        ),
    )(slack, pattern, diagonal, scen_rhs, border, rhs)


def hand_over_kernel(reduced, directions, reduced_out, directions_out):
    reduced_out[...] = reduced[...]
    directions_out[...] = directions[...]


def hand_over(*arrays):
    vmem = pl.BlockSpec(memory_space=pltpu.VMEM)
    return pl.pallas_call(
        hand_over_kernel,
        in_specs=[vmem] * 2,
        out_specs=[vmem] * 2,
        out_shape=tuple(jax.ShapeDtypeStruct(x.shape, x.dtype) for x in arrays),
    )(*arrays)


def per_device(border, pattern, slack, first_diag, rhs, scen_rhs):
    reduced, directions = hand_over(
        *eliminate_panel(slack, pattern, first_diag[None, :], scen_rhs, border, rhs)
    )
    return reduced[None], directions


def solution(mesh):
    return jax.shard_map(
        per_device,
        mesh=mesh,
        in_specs=(
            P("scen", None, "col"),
            P("scen", None, "col"),
            P("scen", None),
            P("col"),
            P("col", None),
            P("scen", "col", None),
        ),
        out_specs=(P("col", "scen", None), P("scen", "col", None)),
        check_vma=False,
    )
```

```python
import functools

import jax
import jax.numpy as jnp
from jax import lax
from jax.experimental import pallas as pl
from jax.experimental.pallas import tpu as pltpu
from jax.sharding import PartitionSpec as P

PW = 512
BLK = 128
HIGHEST = lax.Precision.HIGHEST
MESH = pl.DeviceIdType.MESH
CHUNKS = (9, 7)
STAGES = 2


def dot(a, b, contract=((1,), (0,))):
    return lax.dot_general(
        a, b, (contract, ((), ())), precision=HIGHEST, preferred_element_type=jnp.float32
    )


def halves(x):
    high = x.astype(jnp.bfloat16)
    return high, (x - high.astype(jnp.float32)).astype(jnp.bfloat16)


def blocks_of(steps):
    return [(i, j) for i in range(steps) for j in range(i, steps)]


def invert_factor(block):
    groups = BLK // 8
    shape = (8, BLK)
    sub = lax.broadcasted_iota(jnp.int32, shape, 0)
    lane = lax.broadcasted_iota(jnp.int32, shape, 1)
    rows = [block[8 * i : 8 * i + 8, :] for i in range(groups)]
    inverse = [jnp.where(lane == sub + 8 * i, 1.0, 0.0).astype(jnp.float32) for i in range(groups)]
    for g in range(groups):
        columns = [
            {i: jnp.broadcast_to(rows[i][:, 8 * g + m : 8 * g + m + 1], shape) for i in range(g, groups)}
            for m in range(8)
        ]
        pivots = jnp.ones(shape, jnp.float32)
        for m in range(8):
            head = columns[m][g]
            pivot = jnp.broadcast_to(head[m : m + 1, :], shape)
            scale = 1.0 / pivot
            pivots = jnp.where(sub == m, pivot, pivots)
            row = jnp.broadcast_to(rows[g][m : m + 1, :], shape) * scale
            inverse_row = jnp.broadcast_to(inverse[g][m : m + 1, :], shape) * scale
            factors = [
                jnp.broadcast_to(head[later : later + 1, :], shape) * scale for later in range(m + 1, 8)
            ]
            for i in range(g, groups):
                column = columns[m][i]
                if i == g:
                    column = jnp.where(sub > m, column, 0.0)
                rows[i] = rows[i] - column * row
                inverse[i] = inverse[i] - column * inverse_row
                for later in range(m + 1, 8):
                    columns[later][i] = columns[later][i] - column * factors[later - m - 1]
        inverse[g] = inverse[g] * lax.rsqrt(pivots)
    return jnp.concatenate(inverse, axis=0)


def factor_and_solve(matrix, right, forward, solved, upper, inverses, between):
    steps = matrix.shape[0] // BLK

    def block(i):
        return slice(i * BLK, (i + 1) * BLK)

    def eliminate(j, carry):
        here = pl.ds(pl.multiple_of(j * BLK, BLK), BLK)
        inverse = invert_factor(matrix[here, here])
        inverses[here, :] = inverse
        forward[here, :] = dot(inverse, right[here, :])
        for now in range(steps - 1):
            @pl.when(j == now)
            def _():
                wide = dot(inverse, matrix[block(now), (now + 1) * BLK :])
                upper[block(now), (now + 1) * BLK :] = wide
                for i in range(now + 1, steps):
                    rows = wide[:, (i - now - 1) * BLK : (i - now) * BLK]
                    matrix[block(i), i * BLK :] -= dot(rows, wide[:, (i - now - 1) * BLK :], ((0,), (0,)))
                right[(now + 1) * BLK :, :] -= dot(wide, forward[block(now), :], ((0,), (0,)))
                between(now)
        return carry

    lax.fori_loop(0, steps, eliminate, 0)
    for j in reversed(range(steps)):
        rest = forward[block(j), :]
        if j + 1 < steps:
            rest = rest - dot(upper[block(j), (j + 1) * BLK :], solved[(j + 1) * BLK :, :])
        solved[block(j), :] = dot(inverses[block(j), :], rest, ((0,), (0,)))


def whole_kernel(
    mesh_sizes, slack, pattern, diagonal, scen_rhs, border, rhs, reduced, directions,
    panel, packed, rhs_panel, raw, sent, gram, pair, pieces, lines, matrix, upper, inverses, forward, solved,
    mask, early, stage, high, low, held, split, total, landed, rhs_rows,
    raw_sem, rhs_sem, out_send, out_recv, rhs_send, rhs_recv, rhs_core_send, rhs_core_recv,
    pair_sems, sum_send, sum_recv, chip_send, chip_recv, all_send, all_recv, line_send, line_recv, core_sems,
    stage_sem, own_rhs_sem, send_right, send_left, send_core, recv_right, recv_left, recv_core,
    scen_send, scen_recv,
):
    scen_count, col_count = mesh_sizes
    chips = col_count // 2
    places = scen_count * chips
    scen = lax.axis_index("scen")
    col = lax.axis_index("col")
    chip, core = col // 2, col % 2
    sibling = chip * 2 + (1 - core)
    place = scen * chips + chip
    scen_local, pw, row_share = panel.shape
    row_blocks, width_blocks = pattern.shape[1:]
    row_block = border.shape[1] // row_blocks
    col_block = border.shape[2] // width_blocks
    pivot_width = pw // col_count
    lanes_read = raw.shape[3]
    piece = pieces.shape[1]
    half = piece * places

    def target(t):
        return lax.rem(col + col_count // 2 + t, col_count)

    def rows_of(owner):
        return pl.ds(pl.multiple_of(owner * row_share, row_share), row_share)

    def pivots_of(owner):
        return pl.ds(pl.multiple_of(owner * pivot_width, pivot_width), pivot_width)

    def read(t):
        return pltpu.make_async_copy(
            border.at[:, rows_of(target(t)), pl.ds(0, lanes_read)], raw.at[t], raw_sem.at[t]
        )

    for t in range(col_count):
        read(t).start()
    own_rhs = pltpu.make_async_copy(rhs.at[pl.ds(0, pivot_width)], rhs_panel.at[pivots_of(col)], rhs_sem)
    own_rhs.start()

    own_width = border.shape[2]
    own_share = own_width // scen_count
    bounds = chunk_bounds(rhs.shape[1])
    pieces_per_row = row_share // BLK
    parts = scen_local * pieces_per_row
    blocks = border.shape[1] // row_block
    units = scen_local * blocks
    chip_rows = 2 * scen_local * row_share

    def border_copy(unit):
        scenario, block = unit // blocks, unit % blocks
        slot = unit % STAGES
        return pltpu.make_async_copy(
            border.at[scenario, pl.ds(pl.multiple_of(block * row_block, row_block), row_block)],
            stage.at[slot],
            stage_sem.at[slot],
        )

    for unit in range(STAGES):
        border_copy(unit).start()
    rhs_copy = pltpu.make_async_copy(
        rhs.at[pl.ds(pl.multiple_of(scen * own_share, own_share), own_share)], rhs_rows, own_rhs_sem
    )
    rhs_copy.start()

    def convert(begin, end):
        def body(unit, carry):
            scenario, block = unit // blocks, unit % blocks
            slot = unit % STAGES
            owner = block * row_block // row_share
            place = (owner // 2 * scen_local + scenario) * 2 + owner % 2
            base = place * row_share + block * row_block % row_share
            border_copy(unit).wait()
            weight = mask[scenario, block]

            def some(t, inner):
                value = stage[slot, pl.ds(pl.multiple_of(t * 16, 16), 16), :] * weight
                top = value.astype(jnp.bfloat16)
                here = pl.ds(pl.multiple_of(base + t * 16, 16), 16)
                high[here, :] = top
                low[here, :] = (value - top.astype(jnp.float32)).astype(jnp.bfloat16)
                return inner

            lax.fori_loop(0, row_block // 16, some, 0)

            @pl.when(unit + STAGES < units)
            def _():
                border_copy(unit + STAGES).start()

            return carry

        lax.fori_loop(begin, end, body, 0)

    barrier = pltpu.get_barrier_semaphore()

    def greet(device):
        pl.semaphore_signal(barrier, inc=1, device_id=device, device_id_type=MESH)

    def scen_peer(d):
        return lax.rem(scen + d, scen_count)

    def chip_peer(d):
        return lax.rem(chip + d, chips)

    for d in range(1, scen_count):
        greet({"scen": scen_peer(d)})
    for d in range(1, chips):
        greet({"col": chip_peer(d) * 2 + core})
    for d in range(chips):
        greet({"col": chip_peer(d) * 2 + (1 - core)})

    for s in range(scen_local):
        ones = pattern[s].astype(jnp.float32)
        wide = [jnp.broadcast_to(ones[:, c : c + 1], (row_blocks, col_block)) for c in range(width_blocks)]
        wide = jnp.concatenate(wide, axis=1)
        for r in range(row_blocks):
            mask[s, r] = wide[r : r + 1]

    def hand_out(t):
        return pltpu.make_async_remote_copy(
            src_ref=sent.at[t],
            dst_ref=panel.at[:, pivots_of(col), :],
            send_sem=out_send.at[t],
            recv_sem=out_recv.at[t],
            device_id={"col": target(t)},
            device_id_type=MESH,
        )

    def hand_in(t):
        source = lax.rem(col + 2 * col_count - col_count // 2 - t, col_count)
        return pltpu.make_async_remote_copy(
            src_ref=sent.at[t],
            dst_ref=panel.at[:, pivots_of(source), :],
            send_sem=out_send.at[t],
            recv_sem=out_recv.at[t],
            device_id={"col": source},
            device_id_type=MESH,
        )

    here = col_count - col_count // 2
    for t in range(col_count):
        read(t).wait()
        for s in range(scen_local):
            for r in range(row_share // row_block):
                weight = mask[s, target(t) * (row_share // row_block) + r, :, :lanes_read]
                value = raw[t, s, r * row_block : (r + 1) * row_block, :] * weight
                value = value.T[:pivot_width]
                if t == here:
                    panel[s, pivots_of(col), r * row_block : (r + 1) * row_block] = value
                else:
                    sent[t, s, :, r * row_block : (r + 1) * row_block] = value
        if t == 0:
            pl.semaphore_wait(barrier, scen_count + 2 * chips - 2)
        if t != here:
            hand_out(t).start()

    def rhs_away(e, origin_shift=0):
        return pltpu.make_async_remote_copy(
            src_ref=rhs_panel.at[pivots_of(col)],
            dst_ref=rhs_panel.at[pivots_of(col)],
            send_sem=rhs_send.at[e - 1],
            recv_sem=rhs_recv.at[e - 1],
            device_id={"col": lax.rem(chip + e, chips) * 2 + core},
            device_id_type=MESH,
        )

    def rhs_from(e):
        source = lax.rem(chip + chips - e, chips) * 2 + core
        return pltpu.make_async_remote_copy(
            src_ref=rhs_panel.at[pivots_of(source)],
            dst_ref=rhs_panel.at[pivots_of(source)],
            send_sem=rhs_send.at[e - 1],
            recv_sem=rhs_recv.at[e - 1],
            device_id={"col": source},
            device_id_type=MESH,
        )

    def rhs_core(e, side):
        owner = lax.rem(chip + chips - e, chips) * 2 + side
        return pltpu.make_async_remote_copy(
            src_ref=rhs_panel.at[pivots_of(owner)],
            dst_ref=rhs_panel.at[pivots_of(owner)],
            send_sem=rhs_core_send.at[e],
            recv_sem=rhs_core_recv.at[e],
            device_id={"col": sibling},
            device_id_type=MESH,
        )

    convert(0, units)
    for t in range(col_count):
        if t != here:
            hand_in(t).wait_recv()

    own_rhs.wait()
    for e in range(1, chips):
        rhs_away(e).start()
    rhs_core(0, core).start()

    steps = pw // BLK
    whole = [panel[s] for s in range(scen_local)]
    scaled = [panel[s] / slack[s : s + 1, rows_of(col)] for s in range(scen_local)]
    whole = jnp.concatenate(whole, axis=1)
    scaled = jnp.concatenate(scaled, axis=1)
    row = lax.broadcasted_iota(jnp.int32, (BLK, BLK), 0)
    lane = lax.broadcasted_iota(jnp.int32, (BLK, BLK), 1)
    spots = jnp.concatenate([diagonal[:, :pivot_width]] * (BLK // pivot_width), axis=1)
    index = 0
    for i in range(steps):
        wide = dot(scaled[i * BLK : (i + 1) * BLK], whole[i * BLK :], ((1,), (1,)))
        mine = (row == lane) & ((lane + i * BLK) // pivot_width == col) & (scen == 0)
        for j in range(i, steps):
            value = wide[:, (j - i) * BLK : (j - i + 1) * BLK]
            if i == j:
                value = value + jnp.where(mine, jnp.broadcast_to(spots, (BLK, BLK)), 0.0)
            gram[index * BLK : (index + 1) * BLK, :] = value
            index += 1
    if index * BLK < gram.shape[0]:
        gram[index * BLK :, :] = jnp.zeros((gram.shape[0] - index * BLK, BLK), jnp.float32)

    def half_of(side):
        return pl.ds(pl.multiple_of(side * half, 8), half)

    swap = pltpu.make_async_remote_copy(
        src_ref=gram.at[half_of(1 - core)],
        dst_ref=pair,
        send_sem=pair_sems.at[0],
        recv_sem=pair_sems.at[1],
        device_id={"col": sibling},
        device_id_type=MESH,
    )
    swap.start()
    swap.wait_recv()
    pair[...] += gram[half_of(core), :]

    def piece_of(index):
        return pl.ds(pl.multiple_of(index * piece, 8), piece)

    line = chips * piece

    def line_of(owner, base=0):
        return pl.ds(pl.multiple_of(base + owner * line, 8), line)

    def send(source, into, sends, receives, d, device):
        return pltpu.make_async_remote_copy(
            src_ref=source,
            dst_ref=into,
            send_sem=sends.at[d - 1],
            recv_sem=receives.at[d - 1],
            device_id=device,
            device_id_type=MESH,
        )

    def spread_lines(d):
        source = pair.at[line_of(scen_peer(d))]
        return send(source, lines.at[d - 1], sum_send, sum_recv, d, {"scen": scen_peer(d)})

    def spread(d):
        source = pair.at[piece_of(scen * chips + chip_peer(d))]
        return send(source, pieces.at[d - 1], chip_send, chip_recv, d, {"col": chip_peer(d) * 2 + core})

    for d in range(1, scen_count):
        spread_lines(d).start()
    for e in range(1, chips):
        rhs_from(e).wait_recv()
        rhs_core(e, core).start()
    value = pair[line_of(scen), :]
    for d in range(1, scen_count):
        spread_lines(d).wait_recv()
        value += lines[d - 1]
    pair[line_of(scen), :] = value
    for d in range(1, chips):
        spread(d).start()
    value = pair[piece_of(place), :]
    for d in range(1, chips):
        spread(d).wait_recv()
        value += pieces[d - 1]

    def slot_of(owner):
        return pl.ds(pl.multiple_of(core * half + owner * piece, 8), piece)

    packed[slot_of(place), :] = value

    def collect(d, owner):
        block = packed.at[slot_of(scen * chips + owner)]
        return send(block, block, all_send, all_recv, d, {"col": chip_peer(d) * 2 + core})

    def collect_lines(d, owner):
        block = packed.at[line_of(owner, core * half)]
        return send(block, block, line_send, line_recv, d, {"scen": scen_peer(d)})

    for d in range(1, chips):
        collect(d, chip).start()
    for d in range(1, chips):
        collect(d, chip_peer(chips - d)).wait_recv()
    for d in range(1, scen_count):
        collect_lines(d, scen).start()

    own_slack = [slack[s : s + 1, rows_of(col)] for s in range(scen_local)]

    def hop(q, origin, target, send, recv, lane=core):
        if q == 0:
            block = early.at[origin * 2 + lane]
        else:
            low_row, high_row = bounds[q - 1]
            block = held.at[origin * 2 + lane, 1:, low_row:high_row, :]
        return pltpu.make_async_remote_copy(
            src_ref=block,
            dst_ref=block,
            send_sem=send,
            recv_sem=recv.at[q, origin],
            device_id={"col": target},
            device_id_type=MESH,
        )

    def to_right(q, origin, d=1):
        return hop(q, origin, col + 2 * d, send_right.at[q, origin, d - 1], recv_right)

    def to_left(q, origin, d=1):
        return hop(q, origin, col - 2 * d, send_left.at[q, origin, d - 1], recv_left)

    def to_sibling(q, origin):
        return hop(q, origin, sibling, send_core.at[q, origin], recv_core)

    def from_sibling(q, origin):
        return hop(q, origin, sibling, send_core.at[q, origin], recv_core, 1 - core)

    def send_own(q):
        @pl.when(chip + 1 < chips)
        def _():
            to_right(q, chip).start()

        @pl.when(chip > 0)
        def _():
            to_left(q, chip).start()

        to_sibling(q, chip).start()

    def far_right(d):
        inside = chip + d < chips
        return inside & (chip + d < chips - 1) if d == 2 else inside

    def far_left(d):
        return chip > d if d == 2 else chip >= d

    def send_far(q):
        for d in range(2, chips):
            @pl.when(far_right(d))
            def _():
                to_right(q, chip, d).start()

            @pl.when(far_left(d))
            def _():
                to_left(q, chip, d).start()

    def arrive(q, distance):
        @pl.when(chip >= distance)
        def _():
            origin = chip - distance
            to_right(q, origin).wait_recv()
            if distance == 1:
                @pl.when(chip == chips - 2)
                def _():
                    to_right(q, origin).start()

            to_sibling(q, origin).start()

        @pl.when(chip + distance < chips)
        def _():
            origin = chip + distance
            to_left(q, origin).wait_recv()
            if distance == 1:
                @pl.when(chip == 1)
                def _():
                    to_left(q, origin).start()

            to_sibling(q, origin).start()

        if distance == 1:
            send_far(q)

    def finish(side):
        return pltpu.make_async_remote_copy(
            src_ref=packed.at[half_of(side)],
            dst_ref=packed.at[half_of(side)],
            send_sem=core_sems.at[0],
            recv_sem=core_sems.at[1],
            device_id={"col": sibling},
            device_id_type=MESH,
        )

    early[col] = panel[0, :, :BLK]
    send_own(0)
    for d in range(1, scen_count):
        collect_lines(d, scen_peer(scen_count - d)).wait_recv()
    finish(core).start()
    for e in range(chips):
        rhs_core(e, 1 - core).wait_recv()
    finish(1 - core).wait_recv()
    for t in range(col_count):
        if t != here:
            hand_out(t).wait_send()
    for e in range(1, chips):
        rhs_away(e).wait_send()
    for e in range(chips):
        rhs_core(e, core).wait_send()
    swap.wait_send()
    for d in range(1, chips):
        spread(d).wait_send()
        collect(d, chip).wait_send()
    for d in range(1, scen_count):
        spread_lines(d).wait_send()
        collect_lines(d, scen).wait_send()
    finish(core).wait_send()

    matrix[...] = jnp.zeros_like(matrix)
    for index, (i, j) in enumerate(blocks_of(steps)):
        matrix[i * BLK : (i + 1) * BLK, j * BLK : (j + 1) * BLK] = packed[index * BLK : (index + 1) * BLK, :]
    hops = chips - 1

    def between(step):
        if step == 0 and hops > 0:
            arrive(0, 1)

    factor_and_solve(matrix, rhs_panel, forward, solved, upper, inverses, between)

    def own_rows(q):
        low_row, high_row = bounds[q - 1]
        for s in range(scen_local):
            moved = dot(solved[:, low_row:high_row], panel[s], ((0,), (0,)))
            scaled = moved / own_slack[s]
            for r in range(pieces_per_row):
                held[col, s * pieces_per_row + r, low_row:high_row, :] = scaled[:, r * BLK : (r + 1) * BLK]
            directions[s, :, low_row:high_row] = moved.T

    def early_rows(t):
        owner = lax.rem(col + t, col_count)
        moved = dot(solved[...], early[owner], ((0,), (0,)))
        held[owner, 0] = moved / slack[0:1, pl.ds(pl.multiple_of(owner * row_share, row_share), BLK)]

    width = own_share

    def multiply(q, origin, first, last):
        low_row, high_row = bounds[q - 1]
        count = high_row - low_row
        for k in range(2):
            for part in range(parts):
                top, rest = halves(held[origin * 2 + k, part, low_row:high_row, :])
                s, r = part // pieces_per_row, part % pieces_per_row
                lanes = slice((s * 2 + k) * row_share + r * BLK, (s * 2 + k) * row_share + (r + 1) * BLK)
                split[:count, lanes] = top
                split[count : 2 * count, lanes] = rest
        rows = pl.ds(pl.multiple_of(origin * chip_rows, chip_rows), chip_rows)

        def body(t, carry):
            peer = lax.rem(scen + 1 + t, scen_count)
            lanes = pl.ds(pl.multiple_of(peer * width, width), width)
            both = jnp.dot(split[: 2 * count], high[rows, lanes], preferred_element_type=jnp.float32)
            value = both[:count] + both[count:]
            value += jnp.dot(split[:count], low[rows, lanes], preferred_element_type=jnp.float32)
            if first:
                total[low_row:high_row, lanes] = value
            else:
                total[low_row:high_row, lanes] += value

                @pl.when(last & (t + 1 < scen_count))
                def _():
                    share(q, t + 1).start()

            return carry

        lax.fori_loop(0, scen_count, body, 0)

    def add_in(q, distance):
        if distance == 0:
            from_sibling(q, chip).wait_recv()
            multiply(q, chip, True, False)
            return

        furthest = jnp.maximum(chip, chips - 1 - chip)
        rightmost = chips - 1 - chip == furthest

        @pl.when(chip >= distance)
        def _():
            from_sibling(q, chip - distance).wait_recv()
            multiply(q, chip - distance, False, (distance == furthest) & jnp.logical_not(rightmost))

        @pl.when(chip + distance < chips)
        def _():
            from_sibling(q, chip + distance).wait_recv()
            multiply(q, chip + distance, False, (distance == furthest) & rightmost)

    def share(q, d):
        low_row, high_row = bounds[q - 1]
        peer = lax.rem(scen + d, scen_count)
        return pltpu.make_async_remote_copy(
            src_ref=total.at[low_row:high_row, pl.ds(pl.multiple_of(peer * own_share, own_share), own_share)],
            dst_ref=landed.at[d - 1, low_row:high_row],
            send_sem=scen_send.at[q - 1, d - 1],
            recv_sem=scen_recv.at[q - 1, d - 1],
            device_id={"scen": peer},
            device_id_type=MESH,
        )

    def finish_chunk(q):
        low_row, high_row = bounds[q - 1]
        value = total[low_row:high_row, pl.ds(pl.multiple_of(scen * own_share, own_share), own_share)]
        for d in range(1, scen_count):
            share(q, d).wait_recv()
            value += landed[d - 1, low_row:high_row]
        reduced[:, low_row:high_row] = rhs_rows[:, low_row:high_row] - value.T

    chunks = len(bounds)
    own_rows(1)
    send_own(1)
    for distance in range(2, chips):
        arrive(0, distance)
    for q in range(2, chunks + 1):
        own_rows(q)
    arrive(1, 1)
    if chunks > 1:
        send_own(2)
    for distance in range(chips):
        if distance == 0:
            from_sibling(0, chip).wait_recv()
        else:
            @pl.when(chip >= distance)
            def _():
                from_sibling(0, chip - distance).wait_recv()

            @pl.when(chip + distance < chips)
            def _():
                from_sibling(0, chip + distance).wait_recv()

    def every(t, carry):
        early_rows(t)
        return carry

    lax.fori_loop(1, col_count, every, 0)
    rhs_copy.wait()
    for q in range(1, chunks + 1):
        for distance in range(chips):
            if 2 <= distance + 1 < chips:
                arrive(q, distance + 1)
            if distance == chips - 1 and q < chunks:
                arrive(q + 1, 1)
                if q + 1 < chunks:
                    send_own(q + 2)
            add_in(q, distance)
        if q == 1:
            for s in range(scen_local):
                directions[s] = (scen_rhs[s] - directions[s]) / own_slack[s].T
        else:
            finish_chunk(q - 1)
    finish_chunk(chunks)

    @pl.when(scen == 0)
    def _():
        reduced[:pivot_width, :] = forward[pivots_of(col), :]

    for q in range(chunks + 1):
        @pl.when(chip + 1 < chips)
        def _():
            to_right(q, chip).wait_send()

        @pl.when(chip > 0)
        def _():
            to_left(q, chip).wait_send()

        for d in range(2, chips):
            @pl.when(far_right(d))
            def _():
                to_right(q, chip, d).wait_send()

            @pl.when(far_left(d))
            def _():
                to_left(q, chip, d).wait_send()

        @pl.when((chip == chips - 2) & (chip >= 1))
        def _():
            to_right(q, chip - 1).wait_send()

        @pl.when((chip == 1) & (chip + 1 < chips))
        def _():
            to_left(q, chip + 1).wait_send()

        for origin in range(chips):
            to_sibling(q, origin).wait_send()
        if q > 0:
            for d in range(1, scen_count):
                share(q, d).wait_send()


def chunk_bounds(rhs_count):
    bounds, done = [], 0
    for share in CHUNKS:
        bounds.append((done, done + share * rhs_count // sum(CHUNKS)))
        done += share * rhs_count // sum(CHUNKS)
    return bounds


def eliminate_panel(slack, pattern, diagonal, scen_rhs, border, rhs):
    scen_count = lax.axis_size("scen")
    col_count = lax.axis_size("col")
    chips = col_count // 2
    places = scen_count * chips
    scen_local, row_total, own_width = border.shape
    row_blocks = pattern.shape[1]
    row_share = row_total // col_count
    own_share = own_width // scen_count
    pivot_width = PW // col_count
    rhs_count = rhs.shape[1]
    chunks = len(CHUNKS)
    largest = rhs_count * max(CHUNKS) // sum(CHUNKS)
    lanes_read = -(-pivot_width // BLK) * BLK
    count = len(blocks_of(PW // BLK)) * BLK
    piece = -(-count // (2 * places * 8)) * 8
    half = piece * places
    vmem = pl.BlockSpec(memory_space=pltpu.VMEM)
    hbm = pl.BlockSpec(memory_space=pl.ANY)
    dma = pltpu.SemaphoreType.DMA

    def floats(*shape):
        return pltpu.VMEM(shape, jnp.float32)

    return pl.pallas_call(
        functools.partial(whole_kernel, (scen_count, col_count)),
        in_specs=[vmem] * 4 + [hbm] * 2,
        out_specs=[vmem] * 2,
        out_shape=(
            jax.ShapeDtypeStruct((own_share, rhs_count), jnp.float32),
            jax.ShapeDtypeStruct(scen_rhs.shape, jnp.float32),
        ),
        scratch_shapes=[
            floats(scen_local, PW, row_share),
            floats(2 * half, BLK),
            floats(PW, rhs_count),
            floats(col_count, scen_local, row_share, lanes_read),
            floats(col_count, scen_local, pivot_width, row_share),
            floats(2 * half, BLK),
            floats(half, BLK),
            floats(chips - 1, piece, BLK),
            floats(scen_count - 1, chips * piece, BLK),
            floats(PW, PW),
            floats(PW, PW),
            floats(PW, BLK),
            floats(PW, rhs_count),
            floats(PW, rhs_count),
            floats(scen_local, row_blocks, 1, own_width),
            floats(col_count, PW, BLK),
            floats(STAGES, row_total // row_blocks, own_width),
            pltpu.VMEM((scen_local * row_total, own_width), jnp.bfloat16),
            pltpu.VMEM((scen_local * row_total, own_width), jnp.bfloat16),
            floats(col_count, scen_local * row_share // BLK, rhs_count, BLK),
            pltpu.VMEM((2 * largest, 2 * scen_local * row_share), jnp.bfloat16),
            floats(rhs_count, own_width),
            floats(scen_count - 1, rhs_count, own_share),
            floats(own_share, rhs_count),
            dma((col_count,)),
            dma,
            dma((col_count,)),
            dma((col_count,)),
            dma((chips - 1,)),
            dma((chips - 1,)),
            dma((chips,)),
            dma((chips,)),
            dma((2,)),
            dma((scen_count - 1,)),
            dma((scen_count - 1,)),
            dma((chips - 1,)),
            dma((chips - 1,)),
            dma((chips - 1,)),
            dma((chips - 1,)),
            dma((scen_count - 1,)),
            dma((scen_count - 1,)),
            dma((2,)),
            dma((STAGES,)),
            dma,
            dma((chunks + 1, chips, chips - 1)),
            dma((chunks + 1, chips, chips - 1)),
            dma((chunks + 1, chips)),
            dma((chunks + 1, chips)),
            dma((chunks + 1, chips)),
            dma((chunks + 1, chips)),
            dma((chunks, scen_count - 1)),
            dma((chunks, scen_count - 1)),
        ],
        compiler_params=pltpu.CompilerParams(
            collective_id=0, has_side_effects=True, vmem_limit_bytes=63 << 20
        ),
        cost_estimate=pl.CostEstimate(
            flops=6 * scen_local * row_total * own_width * rhs_count,
            bytes_accessed=4 * scen_local * row_total * own_width,
            transcendentals=0,
        ),
    )(slack, pattern, diagonal, scen_rhs, border, rhs)


def hand_over_kernel(reduced, directions, reduced_out, directions_out):
    reduced_out[...] = reduced[...]
    directions_out[...] = directions[...]


def hand_over(*arrays):
    vmem = pl.BlockSpec(memory_space=pltpu.VMEM)
    return pl.pallas_call(
        hand_over_kernel,
        in_specs=[vmem] * 2,
        out_specs=[vmem] * 2,
        out_shape=tuple(jax.ShapeDtypeStruct(x.shape, x.dtype) for x in arrays),
    )(*arrays)


def per_device(border, pattern, slack, first_diag, rhs, scen_rhs):
    reduced, directions = hand_over(
        *eliminate_panel(slack, pattern, first_diag[None, :], scen_rhs, border, rhs)
    )
    return reduced[None], directions


def solution(mesh):
    return jax.shard_map(
        per_device,
        mesh=mesh,
        in_specs=(
            P("scen", None, "col"),
            P("scen", None, "col"),
            P("scen", None),
            P("col"),
            P("col", None),
            P("scen", "col", None),
        ),
        out_specs=(P("col", "scen", None), P("scen", "col", None)),
        check_vma=False,
    )
```

```python
import functools

import jax
import jax.numpy as jnp
from jax import lax
from jax.experimental import pallas as pl
from jax.experimental.pallas import tpu as pltpu
from jax.sharding import PartitionSpec as P

PW = 512
BLK = 128
HIGHEST = lax.Precision.HIGHEST
MESH = pl.DeviceIdType.MESH
CHUNKS = (9, 7)
STAGES = 2


def dot(a, b, contract=((1,), (0,))):
    return lax.dot_general(
        a, b, (contract, ((), ())), precision=HIGHEST, preferred_element_type=jnp.float32
    )


def halves(x):
    high = x.astype(jnp.bfloat16)
    return high, (x - high.astype(jnp.float32)).astype(jnp.bfloat16)


def blocks_of(steps):
    return [(i, j) for i in range(steps) for j in range(i, steps)]


def invert_factor(block):
    groups = BLK // 8
    shape = (8, BLK)
    sub = lax.broadcasted_iota(jnp.int32, shape, 0)
    lane = lax.broadcasted_iota(jnp.int32, shape, 1)
    rows = [block[8 * i : 8 * i + 8, :] for i in range(groups)]
    inverse = [jnp.where(lane == sub + 8 * i, 1.0, 0.0).astype(jnp.float32) for i in range(groups)]
    for g in range(groups):
        columns = [
            {i: jnp.broadcast_to(rows[i][:, 8 * g + m : 8 * g + m + 1], shape) for i in range(g, groups)}
            for m in range(8)
        ]
        pivots = jnp.ones(shape, jnp.float32)
        for m in range(8):
            head = columns[m][g]
            pivot = jnp.broadcast_to(head[m : m + 1, :], shape)
            scale = 1.0 / pivot
            pivots = jnp.where(sub == m, pivot, pivots)
            row = jnp.broadcast_to(rows[g][m : m + 1, :], shape) * scale
            inverse_row = jnp.broadcast_to(inverse[g][m : m + 1, :], shape) * scale
            factors = [
                jnp.broadcast_to(head[later : later + 1, :], shape) * scale for later in range(m + 1, 8)
            ]
            for i in range(g, groups):
                column = columns[m][i]
                if i == g:
                    column = jnp.where(sub > m, column, 0.0)
                rows[i] = rows[i] - column * row
                inverse[i] = inverse[i] - column * inverse_row
                for later in range(m + 1, 8):
                    columns[later][i] = columns[later][i] - column * factors[later - m - 1]
        inverse[g] = inverse[g] * lax.rsqrt(pivots)
    return jnp.concatenate(inverse, axis=0)


def factor_and_solve(matrix, right, forward, solved, upper, inverses, between):
    steps = matrix.shape[0] // BLK

    def block(i):
        return slice(i * BLK, (i + 1) * BLK)

    def eliminate(j, carry):
        here = pl.ds(pl.multiple_of(j * BLK, BLK), BLK)
        inverse = invert_factor(matrix[here, here])
        inverses[here, :] = inverse
        forward[here, :] = dot(inverse, right[here, :])
        for now in range(steps - 1):
            @pl.when(j == now)
            def _():
                wide = dot(inverse, matrix[block(now), (now + 1) * BLK :])
                upper[block(now), (now + 1) * BLK :] = wide
                for i in range(now + 1, steps):
                    rows = wide[:, (i - now - 1) * BLK : (i - now) * BLK]
                    matrix[block(i), i * BLK :] -= dot(rows, wide[:, (i - now - 1) * BLK :], ((0,), (0,)))
                right[(now + 1) * BLK :, :] -= dot(wide, forward[block(now), :], ((0,), (0,)))
                between(now)
        return carry

    lax.fori_loop(0, steps, eliminate, 0)
    for j in reversed(range(steps)):
        rest = forward[block(j), :]
        if j + 1 < steps:
            rest = rest - dot(upper[block(j), (j + 1) * BLK :], solved[(j + 1) * BLK :, :])
        solved[block(j), :] = dot(inverses[block(j), :], rest, ((0,), (0,)))


def whole_kernel(
    mesh_sizes, slack, pattern, diagonal, scen_rhs, border, rhs, reduced, directions,
    panel, packed, rhs_panel, raw, sent, gram, pair, pieces, lines, matrix, upper, inverses, forward, solved,
    mask, early, stage, high, low, held, split, total, landed, rhs_rows,
    raw_sem, rhs_sem, out_send, out_recv, rhs_send, rhs_recv, rhs_core_send, rhs_core_recv,
    pair_sems, sum_send, sum_recv, chip_send, chip_recv, all_send, all_recv, line_send, line_recv, core_sems,
    stage_sem, own_rhs_sem, send_right, send_left, send_core, recv_right, recv_left, recv_core,
    scen_send, scen_recv,
):
    scen_count, col_count = mesh_sizes
    chips = col_count // 2
    places = scen_count * chips
    scen = lax.axis_index("scen")
    col = lax.axis_index("col")
    chip, core = col // 2, col % 2
    sibling = chip * 2 + (1 - core)
    place = scen * chips + chip
    scen_local, pw, row_share = panel.shape
    row_blocks, width_blocks = pattern.shape[1:]
    row_block = border.shape[1] // row_blocks
    col_block = border.shape[2] // width_blocks
    pivot_width = pw // col_count
    lanes_read = raw.shape[3]
    piece = pieces.shape[1]
    half = piece * places

    def target(t):
        return lax.rem(col + col_count // 2 + t, col_count)

    def rows_of(owner):
        return pl.ds(pl.multiple_of(owner * row_share, row_share), row_share)

    def pivots_of(owner):
        return pl.ds(pl.multiple_of(owner * pivot_width, pivot_width), pivot_width)

    def read(t):
        return pltpu.make_async_copy(
            border.at[:, rows_of(target(t)), pl.ds(0, lanes_read)], raw.at[t], raw_sem.at[t]
        )

    for t in range(col_count):
        read(t).start()
    own_rhs = pltpu.make_async_copy(rhs.at[pl.ds(0, pivot_width)], rhs_panel.at[pivots_of(col)], rhs_sem)
    own_rhs.start()

    own_width = border.shape[2]
    own_share = own_width // scen_count
    bounds = chunk_bounds(rhs.shape[1])
    pieces_per_row = row_share // BLK
    parts = scen_local * pieces_per_row
    blocks = border.shape[1] // row_block
    units = scen_local * blocks
    chip_rows = 2 * scen_local * row_share

    def border_copy(unit):
        scenario, block = unit // blocks, unit % blocks
        slot = unit % STAGES
        return pltpu.make_async_copy(
            border.at[scenario, pl.ds(pl.multiple_of(block * row_block, row_block), row_block)],
            stage.at[slot],
            stage_sem.at[slot],
        )

    for unit in range(STAGES):
        border_copy(unit).start()
    rhs_copy = pltpu.make_async_copy(
        rhs.at[pl.ds(pl.multiple_of(scen * own_share, own_share), own_share)], rhs_rows, own_rhs_sem
    )
    rhs_copy.start()

    def convert(begin, end):
        def body(unit, carry):
            scenario, block = unit // blocks, unit % blocks
            slot = unit % STAGES
            owner = block * row_block // row_share
            place = (owner // 2 * scen_local + scenario) * 2 + owner % 2
            base = place * row_share + block * row_block % row_share
            border_copy(unit).wait()
            weight = mask[scenario, block]

            def some(t, inner):
                value = stage[slot, pl.ds(pl.multiple_of(t * 16, 16), 16), :] * weight
                top = value.astype(jnp.bfloat16)
                here = pl.ds(pl.multiple_of(base + t * 16, 16), 16)
                high[here, :] = top
                low[here, :] = (value - top.astype(jnp.float32)).astype(jnp.bfloat16)
                return inner

            lax.fori_loop(0, row_block // 16, some, 0)

            @pl.when(unit + STAGES < units)
            def _():
                border_copy(unit + STAGES).start()

            return carry

        lax.fori_loop(begin, end, body, 0)

    barrier = pltpu.get_barrier_semaphore()

    def greet(device):
        pl.semaphore_signal(barrier, inc=1, device_id=device, device_id_type=MESH)

    def scen_peer(d):
        return lax.rem(scen + d, scen_count)

    def chip_peer(d):
        return lax.rem(chip + d, chips)

    for d in range(1, scen_count):
        greet({"scen": scen_peer(d)})
    for d in range(1, chips):
        greet({"col": chip_peer(d) * 2 + core})
    for d in range(chips):
        greet({"col": chip_peer(d) * 2 + (1 - core)})

    for s in range(scen_local):
        ones = pattern[s].astype(jnp.float32)
        wide = [jnp.broadcast_to(ones[:, c : c + 1], (row_blocks, col_block)) for c in range(width_blocks)]
        wide = jnp.concatenate(wide, axis=1)
        for r in range(row_blocks):
            mask[s, r] = wide[r : r + 1]

    def hand_out(t):
        return pltpu.make_async_remote_copy(
            src_ref=sent.at[t],
            dst_ref=panel.at[:, pivots_of(col), :],
            send_sem=out_send.at[t],
            recv_sem=out_recv.at[t],
            device_id={"col": target(t)},
            device_id_type=MESH,
        )

    def hand_in(t):
        source = lax.rem(col + 2 * col_count - col_count // 2 - t, col_count)
        return pltpu.make_async_remote_copy(
            src_ref=sent.at[t],
            dst_ref=panel.at[:, pivots_of(source), :],
            send_sem=out_send.at[t],
            recv_sem=out_recv.at[t],
            device_id={"col": source},
            device_id_type=MESH,
        )

    here = col_count - col_count // 2
    for t in range(col_count):
        read(t).wait()
        for s in range(scen_local):
            for r in range(row_share // row_block):
                weight = mask[s, target(t) * (row_share // row_block) + r, :, :lanes_read]
                value = raw[t, s, r * row_block : (r + 1) * row_block, :] * weight
                value = value.T[:pivot_width]
                if t == here:
                    panel[s, pivots_of(col), r * row_block : (r + 1) * row_block] = value
                else:
                    sent[t, s, :, r * row_block : (r + 1) * row_block] = value
        if t == 0:
            pl.semaphore_wait(barrier, scen_count + 2 * chips - 2)
        if t != here:
            hand_out(t).start()

    def rhs_away(e, origin_shift=0):
        return pltpu.make_async_remote_copy(
            src_ref=rhs_panel.at[pivots_of(col)],
            dst_ref=rhs_panel.at[pivots_of(col)],
            send_sem=rhs_send.at[e - 1],
            recv_sem=rhs_recv.at[e - 1],
            device_id={"col": lax.rem(chip + e, chips) * 2 + core},
            device_id_type=MESH,
        )

    def rhs_from(e):
        source = lax.rem(chip + chips - e, chips) * 2 + core
        return pltpu.make_async_remote_copy(
            src_ref=rhs_panel.at[pivots_of(source)],
            dst_ref=rhs_panel.at[pivots_of(source)],
            send_sem=rhs_send.at[e - 1],
            recv_sem=rhs_recv.at[e - 1],
            device_id={"col": source},
            device_id_type=MESH,
        )

    def rhs_core(e, side):
        owner = lax.rem(chip + chips - e, chips) * 2 + side
        return pltpu.make_async_remote_copy(
            src_ref=rhs_panel.at[pivots_of(owner)],
            dst_ref=rhs_panel.at[pivots_of(owner)],
            send_sem=rhs_core_send.at[e],
            recv_sem=rhs_core_recv.at[e],
            device_id={"col": sibling},
            device_id_type=MESH,
        )

    convert(0, units)
    for t in range(col_count):
        if t != here:
            hand_in(t).wait_recv()

    own_rhs.wait()
    for e in range(1, chips):
        rhs_away(e).start()
    rhs_core(0, core).start()

    steps = pw // BLK
    whole = [panel[s] for s in range(scen_local)]
    scaled = [panel[s] / slack[s : s + 1, rows_of(col)] for s in range(scen_local)]
    whole = jnp.concatenate(whole, axis=1)
    scaled = jnp.concatenate(scaled, axis=1)
    row = lax.broadcasted_iota(jnp.int32, (BLK, BLK), 0)
    lane = lax.broadcasted_iota(jnp.int32, (BLK, BLK), 1)
    spots = jnp.concatenate([diagonal[:, :pivot_width]] * (BLK // pivot_width), axis=1)
    index = 0
    for i in range(steps):
        wide = dot(scaled[i * BLK : (i + 1) * BLK], whole[i * BLK :], ((1,), (1,)))
        mine = (row == lane) & ((lane + i * BLK) // pivot_width == col) & (scen == 0)
        for j in range(i, steps):
            value = wide[:, (j - i) * BLK : (j - i + 1) * BLK]
            if i == j:
                value = value + jnp.where(mine, jnp.broadcast_to(spots, (BLK, BLK)), 0.0)
            gram[index * BLK : (index + 1) * BLK, :] = value
            index += 1
    if index * BLK < gram.shape[0]:
        gram[index * BLK :, :] = jnp.zeros((gram.shape[0] - index * BLK, BLK), jnp.float32)

    def half_of(side):
        return pl.ds(pl.multiple_of(side * half, 8), half)

    swap = pltpu.make_async_remote_copy(
        src_ref=gram.at[half_of(1 - core)],
        dst_ref=pair,
        send_sem=pair_sems.at[0],
        recv_sem=pair_sems.at[1],
        device_id={"col": sibling},
        device_id_type=MESH,
    )
    swap.start()
    swap.wait_recv()
    pair[...] += gram[half_of(core), :]

    def piece_of(index):
        return pl.ds(pl.multiple_of(index * piece, 8), piece)

    line = chips * piece

    def line_of(owner, base=0):
        return pl.ds(pl.multiple_of(base + owner * line, 8), line)

    def send(source, into, sends, receives, d, device):
        return pltpu.make_async_remote_copy(
            src_ref=source,
            dst_ref=into,
            send_sem=sends.at[d - 1],
            recv_sem=receives.at[d - 1],
            device_id=device,
            device_id_type=MESH,
        )

    def spread_lines(d):
        source = pair.at[line_of(scen_peer(d))]
        return send(source, lines.at[d - 1], sum_send, sum_recv, d, {"scen": scen_peer(d)})

    def spread(d):
        source = pair.at[piece_of(scen * chips + chip_peer(d))]
        return send(source, pieces.at[d - 1], chip_send, chip_recv, d, {"col": chip_peer(d) * 2 + core})

    for d in range(1, scen_count):
        spread_lines(d).start()
    for e in range(1, chips):
        rhs_from(e).wait_recv()
        rhs_core(e, core).start()
    value = pair[line_of(scen), :]
    for d in range(1, scen_count):
        spread_lines(d).wait_recv()
        value += lines[d - 1]
    pair[line_of(scen), :] = value
    for d in range(1, chips):
        spread(d).start()
    value = pair[piece_of(place), :]
    for d in range(1, chips):
        spread(d).wait_recv()
        value += pieces[d - 1]

    def slot_of(owner):
        return pl.ds(pl.multiple_of(core * half + owner * piece, 8), piece)

    packed[slot_of(place), :] = value

    def collect(d, owner):
        block = packed.at[slot_of(scen * chips + owner)]
        return send(block, block, all_send, all_recv, d, {"col": chip_peer(d) * 2 + core})

    def collect_lines(d, owner):
        block = packed.at[line_of(owner, core * half)]
        return send(block, block, line_send, line_recv, d, {"scen": scen_peer(d)})

    for d in range(1, chips):
        collect(d, chip).start()
    for d in range(1, chips):
        collect(d, chip_peer(chips - d)).wait_recv()
    for d in range(1, scen_count):
        collect_lines(d, scen).start()

    own_slack = [slack[s : s + 1, rows_of(col)] for s in range(scen_local)]

    def hop(q, origin, target, send, recv, lane=core):
        if q == 0:
            block = early.at[origin * 2 + lane]
        else:
            low_row, high_row = bounds[q - 1]
            block = held.at[origin * 2 + lane, 1:, low_row:high_row, :]
        return pltpu.make_async_remote_copy(
            src_ref=block,
            dst_ref=block,
            send_sem=send,
            recv_sem=recv.at[q, origin],
            device_id={"col": target},
            device_id_type=MESH,
        )

    def to_right(q, origin, d=1):
        return hop(q, origin, col + 2 * d, send_right.at[q, origin, d - 1], recv_right)

    def to_left(q, origin, d=1):
        return hop(q, origin, col - 2 * d, send_left.at[q, origin, d - 1], recv_left)

    def to_sibling(q, origin):
        return hop(q, origin, sibling, send_core.at[q, origin], recv_core)

    def from_sibling(q, origin):
        return hop(q, origin, sibling, send_core.at[q, origin], recv_core, 1 - core)

    def send_own(q):
        @pl.when(chip + 1 < chips)
        def _():
            to_right(q, chip).start()

        @pl.when(chip > 0)
        def _():
            to_left(q, chip).start()

        to_sibling(q, chip).start()

    def far_right(d):
        inside = chip + d < chips
        return inside & (chip + d < chips - 1) if d == 2 else inside

    def far_left(d):
        return chip > d if d == 2 else chip >= d

    def send_far(q):
        for d in range(2, chips):
            @pl.when(far_right(d))
            def _():
                to_right(q, chip, d).start()

            @pl.when(far_left(d))
            def _():
                to_left(q, chip, d).start()

    def arrive(q, distance):
        @pl.when(chip >= distance)
        def _():
            origin = chip - distance
            to_right(q, origin).wait_recv()
            if distance == 1:
                @pl.when(chip == chips - 2)
                def _():
                    to_right(q, origin).start()

            to_sibling(q, origin).start()

        @pl.when(chip + distance < chips)
        def _():
            origin = chip + distance
            to_left(q, origin).wait_recv()
            if distance == 1:
                @pl.when(chip == 1)
                def _():
                    to_left(q, origin).start()

            to_sibling(q, origin).start()

        if distance == 1:
            send_far(q)

    def finish(side):
        return pltpu.make_async_remote_copy(
            src_ref=packed.at[half_of(side)],
            dst_ref=packed.at[half_of(side)],
            send_sem=core_sems.at[0],
            recv_sem=core_sems.at[1],
            device_id={"col": sibling},
            device_id_type=MESH,
        )

    early[col] = panel[0, :, :BLK]
    send_own(0)
    for d in range(1, scen_count):
        collect_lines(d, scen_peer(scen_count - d)).wait_recv()
    finish(core).start()
    for e in range(chips):
        rhs_core(e, 1 - core).wait_recv()
    finish(1 - core).wait_recv()
    for t in range(col_count):
        if t != here:
            hand_out(t).wait_send()
    for e in range(1, chips):
        rhs_away(e).wait_send()
    for e in range(chips):
        rhs_core(e, core).wait_send()
    swap.wait_send()
    for d in range(1, chips):
        spread(d).wait_send()
        collect(d, chip).wait_send()
    for d in range(1, scen_count):
        spread_lines(d).wait_send()
        collect_lines(d, scen).wait_send()
    finish(core).wait_send()

    for index, (i, j) in enumerate(blocks_of(steps)):
        matrix[i * BLK : (i + 1) * BLK, j * BLK : (j + 1) * BLK] = packed[index * BLK : (index + 1) * BLK, :]
    hops = chips - 1

    def between(step):
        if step == 0 and hops > 0:
            arrive(0, 1)

    factor_and_solve(matrix, rhs_panel, forward, solved, upper, inverses, between)

    def own_rows(q):
        low_row, high_row = bounds[q - 1]
        for s in range(scen_local):
            moved = dot(solved[:, low_row:high_row], panel[s], ((0,), (0,)))
            scaled = moved / own_slack[s]
            for r in range(pieces_per_row):
                held[col, s * pieces_per_row + r, low_row:high_row, :] = scaled[:, r * BLK : (r + 1) * BLK]

    def early_rows(t):
        owner = lax.rem(col + t, col_count)
        moved = dot(solved[...], early[owner], ((0,), (0,)))
        held[owner, 0] = moved / slack[0:1, pl.ds(pl.multiple_of(owner * row_share, row_share), BLK)]

    width = own_share

    def multiply(q, origin, first, last):
        low_row, high_row = bounds[q - 1]
        count = high_row - low_row
        for k in range(2):
            for part in range(parts):
                top, rest = halves(held[origin * 2 + k, part, low_row:high_row, :])
                s, r = part // pieces_per_row, part % pieces_per_row
                lanes = slice((s * 2 + k) * row_share + r * BLK, (s * 2 + k) * row_share + (r + 1) * BLK)
                split[:count, lanes] = top
                split[count : 2 * count, lanes] = rest
        rows = pl.ds(pl.multiple_of(origin * chip_rows, chip_rows), chip_rows)

        def body(t, carry):
            peer = lax.rem(scen + 1 + t, scen_count)
            lanes = pl.ds(pl.multiple_of(peer * width, width), width)
            both = jnp.dot(split[: 2 * count], high[rows, lanes], preferred_element_type=jnp.float32)
            value = both[:count] + both[count:]
            value += jnp.dot(split[:count], low[rows, lanes], preferred_element_type=jnp.float32)
            if first:
                total[low_row:high_row, lanes] = value
            else:
                total[low_row:high_row, lanes] += value

                @pl.when(last & (t + 1 < scen_count))
                def _():
                    share(q, t + 1).start()

            return carry

        lax.fori_loop(0, scen_count, body, 0)

    def add_in(q, distance):
        if distance == 0:
            from_sibling(q, chip).wait_recv()
            multiply(q, chip, True, False)
            return

        furthest = jnp.maximum(chip, chips - 1 - chip)
        rightmost = chips - 1 - chip == furthest

        @pl.when(chip >= distance)
        def _():
            from_sibling(q, chip - distance).wait_recv()
            multiply(q, chip - distance, False, (distance == furthest) & jnp.logical_not(rightmost))

        @pl.when(chip + distance < chips)
        def _():
            from_sibling(q, chip + distance).wait_recv()
            multiply(q, chip + distance, False, (distance == furthest) & rightmost)

    def share(q, d):
        low_row, high_row = bounds[q - 1]
        peer = lax.rem(scen + d, scen_count)
        return pltpu.make_async_remote_copy(
            src_ref=total.at[low_row:high_row, pl.ds(pl.multiple_of(peer * own_share, own_share), own_share)],
            dst_ref=landed.at[d - 1, low_row:high_row],
            send_sem=scen_send.at[q - 1, d - 1],
            recv_sem=scen_recv.at[q - 1, d - 1],
            device_id={"scen": peer},
            device_id_type=MESH,
        )

    def finish_chunk(q):
        low_row, high_row = bounds[q - 1]
        value = total[low_row:high_row, pl.ds(pl.multiple_of(scen * own_share, own_share), own_share)]
        for d in range(1, scen_count):
            share(q, d).wait_recv()
            value += landed[d - 1, low_row:high_row]
        reduced[:, low_row:high_row] = rhs_rows[:, low_row:high_row] - value.T

    chunks = len(bounds)
    own_rows(1)
    send_own(1)
    for distance in range(2, chips):
        arrive(0, distance)
    for q in range(2, chunks + 1):
        own_rows(q)
    arrive(1, 1)
    if chunks > 1:
        send_own(2)
    for distance in range(chips):
        if distance == 0:
            from_sibling(0, chip).wait_recv()
        else:
            @pl.when(chip >= distance)
            def _():
                from_sibling(0, chip - distance).wait_recv()

            @pl.when(chip + distance < chips)
            def _():
                from_sibling(0, chip + distance).wait_recv()

    def every(t, carry):
        early_rows(t)
        return carry

    lax.fori_loop(1, col_count, every, 0)
    rhs_copy.wait()
    for q in range(1, chunks + 1):
        for distance in range(chips):
            if 2 <= distance + 1 < chips:
                arrive(q, distance + 1)
            if distance == chips - 1 and q < chunks:
                arrive(q + 1, 1)
                if q + 1 < chunks:
                    send_own(q + 2)
            add_in(q, distance)
        if q == 1:
            for s in range(scen_local):
                scaled = [held[col, s * pieces_per_row + r].T for r in range(pieces_per_row)]
                directions[s] = scen_rhs[s] / own_slack[s].T - jnp.concatenate(scaled, axis=0)
        else:
            finish_chunk(q - 1)
    finish_chunk(chunks)

    @pl.when(scen == 0)
    def _():
        reduced[:pivot_width, :] = forward[pivots_of(col), :]

    for q in range(chunks + 1):
        @pl.when(chip + 1 < chips)
        def _():
            to_right(q, chip).wait_send()

        @pl.when(chip > 0)
        def _():
            to_left(q, chip).wait_send()

        for d in range(2, chips):
            @pl.when(far_right(d))
            def _():
                to_right(q, chip, d).wait_send()

            @pl.when(far_left(d))
            def _():
                to_left(q, chip, d).wait_send()

        @pl.when((chip == chips - 2) & (chip >= 1))
        def _():
            to_right(q, chip - 1).wait_send()

        @pl.when((chip == 1) & (chip + 1 < chips))
        def _():
            to_left(q, chip + 1).wait_send()

        for origin in range(chips):
            to_sibling(q, origin).wait_send()
        if q > 0:
            for d in range(1, scen_count):
                share(q, d).wait_send()


def chunk_bounds(rhs_count):
    bounds, done = [], 0
    for share in CHUNKS:
        bounds.append((done, done + share * rhs_count // sum(CHUNKS)))
        done += share * rhs_count // sum(CHUNKS)
    return bounds


def eliminate_panel(slack, pattern, diagonal, scen_rhs, border, rhs):
    scen_count = lax.axis_size("scen")
    col_count = lax.axis_size("col")
    chips = col_count // 2
    places = scen_count * chips
    scen_local, row_total, own_width = border.shape
    row_blocks = pattern.shape[1]
    row_share = row_total // col_count
    own_share = own_width // scen_count
    pivot_width = PW // col_count
    rhs_count = rhs.shape[1]
    chunks = len(CHUNKS)
    largest = rhs_count * max(CHUNKS) // sum(CHUNKS)
    lanes_read = -(-pivot_width // BLK) * BLK
    count = len(blocks_of(PW // BLK)) * BLK
    piece = -(-count // (2 * places * 8)) * 8
    half = piece * places
    vmem = pl.BlockSpec(memory_space=pltpu.VMEM)
    hbm = pl.BlockSpec(memory_space=pl.ANY)
    dma = pltpu.SemaphoreType.DMA

    def floats(*shape):
        return pltpu.VMEM(shape, jnp.float32)

    return pl.pallas_call(
        functools.partial(whole_kernel, (scen_count, col_count)),
        in_specs=[vmem] * 4 + [hbm] * 2,
        out_specs=[vmem] * 2,
        out_shape=(
            jax.ShapeDtypeStruct((own_share, rhs_count), jnp.float32),
            jax.ShapeDtypeStruct(scen_rhs.shape, jnp.float32),
        ),
        scratch_shapes=[
            floats(scen_local, PW, row_share),
            floats(2 * half, BLK),
            floats(PW, rhs_count),
            floats(col_count, scen_local, row_share, lanes_read),
            floats(col_count, scen_local, pivot_width, row_share),
            floats(2 * half, BLK),
            floats(half, BLK),
            floats(chips - 1, piece, BLK),
            floats(scen_count - 1, chips * piece, BLK),
            floats(PW, PW),
            floats(PW, PW),
            floats(PW, BLK),
            floats(PW, rhs_count),
            floats(PW, rhs_count),
            floats(scen_local, row_blocks, 1, own_width),
            floats(col_count, PW, BLK),
            floats(STAGES, row_total // row_blocks, own_width),
            pltpu.VMEM((scen_local * row_total, own_width), jnp.bfloat16),
            pltpu.VMEM((scen_local * row_total, own_width), jnp.bfloat16),
            floats(col_count, scen_local * row_share // BLK, rhs_count, BLK),
            pltpu.VMEM((2 * largest, 2 * scen_local * row_share), jnp.bfloat16),
            floats(rhs_count, own_width),
            floats(scen_count - 1, rhs_count, own_share),
            floats(own_share, rhs_count),
            dma((col_count,)),
            dma,
            dma((col_count,)),
            dma((col_count,)),
            dma((chips - 1,)),
            dma((chips - 1,)),
            dma((chips,)),
            dma((chips,)),
            dma((2,)),
            dma((scen_count - 1,)),
            dma((scen_count - 1,)),
            dma((chips - 1,)),
            dma((chips - 1,)),
            dma((chips - 1,)),
            dma((chips - 1,)),
            dma((scen_count - 1,)),
            dma((scen_count - 1,)),
            dma((2,)),
            dma((STAGES,)),
            dma,
            dma((chunks + 1, chips, chips - 1)),
            dma((chunks + 1, chips, chips - 1)),
            dma((chunks + 1, chips)),
            dma((chunks + 1, chips)),
            dma((chunks + 1, chips)),
            dma((chunks + 1, chips)),
            dma((chunks, scen_count - 1)),
            dma((chunks, scen_count - 1)),
        ],
        compiler_params=pltpu.CompilerParams(
            collective_id=0, has_side_effects=True, vmem_limit_bytes=63 << 20
        ),
        cost_estimate=pl.CostEstimate(
            flops=6 * scen_local * row_total * own_width * rhs_count,
            bytes_accessed=4 * scen_local * row_total * own_width,
            transcendentals=0,
        ),
    )(slack, pattern, diagonal, scen_rhs, border, rhs)


def hand_over_kernel(*refs):
    count = len(refs) // 3
    sources, outs, held, sems = refs[:count], refs[count : 2 * count], refs[2 * count : 3 * count], refs[-1]
    reads = [pltpu.make_async_copy(x, y, sems.at[0, i]) for i, (x, y) in enumerate(zip(sources, held))]
    writes = [pltpu.make_async_copy(x, y, sems.at[1, i]) for i, (x, y) in enumerate(zip(held, outs))]
    for read in reads:
        read.start()
    for read, write in zip(reads, writes):
        read.wait()
        write.start()
    for write in writes:
        write.wait()


def hand_over(*arrays):
    hbm = pl.BlockSpec(memory_space=pl.ANY)
    return pl.pallas_call(
        hand_over_kernel,
        in_specs=[hbm] * len(arrays),
        out_specs=[hbm] * len(arrays),
        out_shape=tuple(jax.ShapeDtypeStruct(x.shape, x.dtype) for x in arrays),
        scratch_shapes=[pltpu.VMEM(x.shape, x.dtype) for x in arrays]
        + [pltpu.SemaphoreType.DMA((2, len(arrays)))],
    )(*arrays)


def per_device(border, pattern, slack, first_diag, rhs, scen_rhs):
    reduced, directions = hand_over(
        *eliminate_panel(slack, pattern, first_diag[None, :], scen_rhs, border, rhs)
    )
    return reduced[None], directions


def solution(mesh):
    return jax.shard_map(
        per_device,
        mesh=mesh,
        in_specs=(
            P("scen", None, "col"),
            P("scen", None, "col"),
            P("scen", None),
            P("col"),
            P("col", None),
            P("scen", "col", None),
        ),
        out_specs=(P("col", "scen", None), P("scen", "col", None)),
        check_vma=False,
    )
```
